32 devices in a mesh: ctx: 8 (over z, y), head: 4 (over x, core).
Axes of the slice: x: 2, y: 2, z: 4, core: 2. Of those that a mesh axis runs over, the one named last changes fastest.
Arguments:
- queries: bfloat16 [4096, 16, 128], P('ctx', 'head'), may hold values from -16 to 16
- keys: bfloat16 [4096, 1, 128], P('ctx'), may hold values from -6 to 6
- values: bfloat16 [4096, 1, 128], P('ctx'), may hold values from -6 to 6
- d_out: bfloat16 [4096, 16, 128], P('ctx', 'head'), may hold values from -1.796875 to 1.796875
- block_pos: int32 [4, 8], replicated, may hold values from 0 to 7, each once within a row
- block_mask: int32 [4, 8, 8], replicated, may hold values 0 or 1
Outputs:
- d_queries: bfloat16 [4096, 16, 128], P('ctx', 'head')
- d_keys: bfloat16 [4096, 1, 128], P('ctx')
- d_values: bfloat16 [4096, 1, 128], P('ctx')
The draws below stay inside these ranges and needn't reach their ends.
Inputs may be any that keep to these rules, and one draw needn't show every extreme that they name: `block_pos`: each row holds each of the 8 block numbers once. `block_mask`: only entries [s, i, i2] with i2 < i are read.
All inputs are finite; a program needn't handle non-finite values.
Results may differ from the reference program's by a relative error of at most 0.0075.
Values may be sent and summed in bfloat16 or wider, within the bound.
No kernel may reach another device: no remote copies, remote signals or barrier semaphores. Data moves between devices by JAX's collectives and lax.ppermute only.
A program may use at most 64 MiB of HBM per device.

```python
import jax
import jax.numpy as jnp
from jax import lax

HD = 128
GROUP = 16
BLK = 128
SEQS = 4
QB_DEV = 4
HQ = 16
KVH = 1
TOKENS = 4096
LEN = 1024
NBLK = 8
N_CTX = 8


def query_key_pair(key):
    base = jax.random.fold_in(key, 7101)
    first, second = jax.random.split(base, 2)
    query_draw = jnp.clip(jax.random.normal(first, (TOKENS, HQ, HD), jnp.float32), -4.5, 4.5)
    key_draw = jnp.clip(jax.random.normal(second, (TOKENS, KVH, HD), jnp.float32), -4.5, 4.5)
    return (query_draw, key_draw)


def draw_queries(key, part):
    return query_key_pair(key)[0].astype(jnp.bfloat16)


def draw_keys(key, part):
    return query_key_pair(key)[1].astype(jnp.bfloat16)


def with_ends(values, key, low, top_value):
    index_at = [jax.random.randint(jax.random.fold_in(key, axis), (), 0, length) for axis, length in enumerate(values.shape)]
    longest = values.shape.index(max(values.shape))
    beside = index_at[:longest] + [(index_at[longest] + 1) % values.shape[longest]] + index_at[longest + 1:]
    return values.at[tuple(index_at)].set(low).at[tuple(beside)].set(top_value)


def block_levels(key, dims, shards, least, high):
    def one(position, blocks):
        draws = jax.random.uniform(jax.random.fold_in(jax.random.fold_in(key, 6), position), (blocks,), jnp.float32, least / len(shards), high / len(shards))
        return jnp.repeat(jnp.exp(draws), dims[position] // blocks).reshape((-1,) + (1,) * (len(dims) - position - 1))

    gain = one(*shards[0])
    for cut in shards[1:]:
        gain = gain * one(*cut)
    return gain


def gaussian(rng, shape, spread, most, cuts=(), kind=jnp.bfloat16):
    values = spread * jax.random.normal(rng, shape, jnp.float32)
    if cuts:
        values = values * block_levels(rng, shape, cuts, -0.22, 0.18)
    return jnp.clip(values, -most, most).astype(kind)


def setup_inputs(seed: int = 0) -> dict:
    key_of = jax.random.split(jax.random.key(seed), 7)
    return {
        "queries": draw_queries(jax.random.fold_in(key_of[6], 71), 0),
        "keys": draw_keys(jax.random.fold_in(key_of[6], 71), 0),
        "values": gaussian(key_of[2], (TOKENS, KVH, HD), 1.0, 6.0, ((0, 8),)),
        "d_out": gaussian(key_of[3], (TOKENS, HQ, HD), 0.3, 1.796875, ((0, 8), (1, 4))),
        "block_pos": jax.vmap(lambda own: jax.random.permutation(own, NBLK))(jax.random.split(key_of[4], SEQS)).reshape((SEQS, NBLK)).astype(jnp.int32),
        "block_mask": with_ends((jax.random.randint(key_of[5], (SEQS, NBLK, NBLK), 0, 2) < 1).astype(jnp.int32), jax.random.fold_in(key_of[5], 1), 0, 1),
    }


def contract_rows(left, right):
    return jnp.dot(left, right.T, preferred_element_type=jnp.float32)


def to_sequences(stored, members):
    width = stored.shape[1]
    depth = stored.shape[2]
    grouped = stored.reshape(members, SEQS, QB_DEV * BLK, width, depth)
    return jnp.transpose(grouped, (1, 0, 2, 3, 4)).reshape(SEQS, LEN, width, depth)


def to_stored(ordered, members):
    width = ordered.shape[2]
    depth = ordered.shape[3]
    grouped = ordered.reshape(SEQS, members, QB_DEV * BLK, width, depth)
    return jnp.transpose(grouped, (1, 0, 2, 3, 4)).reshape(TOKENS, width, depth)


def reference(queries, keys, values, d_out, block_pos, block_mask):
    members = N_CTX // SEQS
    score_scale = HD ** -0.5
    block_rows = BLK * GROUP

    def head_groups(stored):
        ordered = to_sequences(stored, members).reshape(SEQS, LEN, KVH, GROUP, HD)
        return jnp.transpose(ordered, (0, 2, 1, 3, 4)).reshape(SEQS * KVH, LEN * GROUP, HD)

    def kv_groups(stored):
        ordered = to_sequences(stored, members)
        return jnp.transpose(ordered, (0, 2, 1, 3)).reshape(SEQS * KVH, LEN, HD)

    operands = (head_groups(queries), head_groups(d_out), kv_groups(keys), kv_groups(values),
                jnp.repeat(block_pos, KVH, axis=0), jnp.repeat(block_mask, KVH, axis=0))

    def one_group(group_operands):
        query_rows, grad_rows, key_rows, value_rows, order, mask_table = group_operands

        def visible(query_slot, key_slot):
            query_block = order[query_slot]
            key_block = order[key_slot]
            earlier = jnp.logical_and(key_block < query_block, mask_table[query_block, key_block] == 1)
            return jnp.logical_or(query_slot == key_slot, earlier)

        def row_slice(array, slot, count):
            return lax.dynamic_slice_in_dim(array, (slot * count).astype(jnp.int32), count, 0)

        def logits_of(query_slot, key_slot):
            q_block = row_slice(query_rows, query_slot, block_rows)
            k_block = row_slice(key_rows, key_slot, BLK)
            logits = contract_rows(q_block, k_block) * score_scale
            query_token = lax.broadcasted_iota(jnp.int32, logits.shape, 0) // GROUP
            key_token = lax.broadcasted_iota(jnp.int32, logits.shape, 1)
            allowed = jnp.logical_or(query_slot != key_slot, key_token <= query_token)
            return jnp.where(allowed, logits, -jnp.inf)

        def stats_block(query_slot):
            g_block = row_slice(grad_rows, query_slot, block_rows)

            def visit(key_slot, running):
                def update(running):
                    maxima, totals, weighted = running
                    logits = logits_of(query_slot, key_slot)
                    v_block = row_slice(value_rows, key_slot, BLK)
                    dprob_rows = contract_rows(g_block, v_block)
                    new_max = jnp.maximum(maxima, jnp.max(logits, axis=1))
                    factor = jnp.exp(maxima - new_max)
                    exp_rows = jnp.exp(logits - new_max[:, None])
                    return (new_max, totals * factor + jnp.sum(exp_rows, axis=1),
                            weighted * factor + jnp.sum(exp_rows * dprob_rows, axis=1))
                return lax.cond(visible(query_slot, key_slot), update, lambda kept: kept, running)

            initial = (jnp.full((block_rows,), -jnp.inf, jnp.float32), jnp.zeros((block_rows,), jnp.float32),
                       jnp.zeros((block_rows,), jnp.float32))
            maxima, totals, weighted = lax.fori_loop(0, NBLK, visit, initial)
            return maxima + jnp.log(totals), weighted / totals

        log_sums, deltas = lax.map(stats_block, jnp.arange(NBLK, dtype=jnp.int32))

        def grad_block(key_sums, query_slot):
            q_block = row_slice(query_rows, query_slot, block_rows)
            g_block = row_slice(grad_rows, query_slot, block_rows)
            log_row = log_sums[query_slot]
            delta_row = deltas[query_slot]

            def visit(key_slot, running):
                def update(running):
                    query_grad, key_sums = running
                    logits = logits_of(query_slot, key_slot)
                    k_block = row_slice(key_rows, key_slot, BLK)
                    v_block = row_slice(value_rows, key_slot, BLK)
                    prob_rows = jnp.exp(logits - log_row[:, None])
                    dprob_rows = contract_rows(g_block, v_block)
                    dscore = (prob_rows * (dprob_rows - delta_row[:, None])).astype(jnp.bfloat16)
                    query_grad = query_grad + jnp.dot(dscore, k_block, preferred_element_type=jnp.float32)
                    key_add = jnp.dot(dscore.T, q_block, preferred_element_type=jnp.float32)
                    value_add = jnp.dot(prob_rows.astype(jnp.bfloat16).T, g_block, preferred_element_type=jnp.float32)
                    key_start = (key_slot * BLK).astype(jnp.int32)
                    previous = lax.dynamic_slice_in_dim(key_sums, key_start, BLK, 1)
                    key_sums = lax.dynamic_update_slice_in_dim(key_sums, previous + jnp.stack([key_add, value_add]), key_start, 1)
                    return query_grad, key_sums
                return lax.cond(visible(query_slot, key_slot), update, lambda kept: kept, running)

            query_grad, key_sums = lax.fori_loop(0, NBLK, visit, (jnp.zeros((block_rows, HD), jnp.float32), key_sums))
            return key_sums, query_grad

        key_sums, query_grads = lax.scan(grad_block, jnp.zeros((2, LEN, HD), jnp.float32), jnp.arange(NBLK, dtype=jnp.int32))
        d_query = (query_grads.reshape(LEN * GROUP, HD) * score_scale).astype(jnp.bfloat16)
        d_key = (key_sums[0] * score_scale).astype(jnp.bfloat16)
        d_value = key_sums[1].astype(jnp.bfloat16)
        return d_query, d_key, d_value

    query_out, key_out, value_out = lax.map(one_group, operands)
    query_seq = jnp.transpose(query_out.reshape(SEQS, KVH, LEN, GROUP, HD), (0, 2, 1, 3, 4)).reshape(SEQS, LEN, HQ, HD)
    key_seq = jnp.transpose(key_out.reshape(SEQS, KVH, LEN, HD), (0, 2, 1, 3))
    value_seq = jnp.transpose(value_out.reshape(SEQS, KVH, LEN, HD), (0, 2, 1, 3))
    return to_stored(query_seq, members), to_stored(key_seq, members), to_stored(value_seq, members)
```

```python
import functools

import jax
import jax.numpy as jnp
from jax import lax
from jax.experimental import pallas as pl
from jax.experimental.pallas import tpu as pltpu
from jax.sharding import PartitionSpec as P

GROUP = 16
BLK = 128
SEQS = 4
LOG2E = 1.4426950408889634
MASKED = -1e30
SUB = 8


def dot_nt(left, right):
    return lax.dot_general(
        left, right, (((1,), (1,)), ((), ())), preferred_element_type=jnp.float32
    )


def dot_nn(left, right):
    return lax.dot_general(
        left, right, (((1,), (0,)), ((), ())), preferred_element_type=jnp.float32
    )


def by_sublane(value):
    return value.reshape(value.shape[0] // SUB, SUB, value.shape[1])


def shifted(value, axis, steps):
    count = lax.axis_size(axis)
    return lax.ppermute(value, axis, [(i, (i + steps) % count) for i in range(count)])


def swapped(value, axis, bit):
    count = lax.axis_size(axis)
    return lax.ppermute(value, axis, [(i, i ^ bit) for i in range(count)])


class Shape:
    def __init__(self, tokens, heads, depth, members):
        self.tokens = tokens
        self.heads = heads
        self.depth = depth
        self.members = members
        self.blocks = tokens // BLK
        self.rows = BLK * heads
        self.scale = depth**-0.5


def place(dims):
    ctx = lax.axis_index("ctx")
    return ctx % SEQS, ctx // SEQS


def seen(dims, pos_ref, mask_ref, query_slot, hop, key_slot):
    seq, member = place(dims)
    owner = (member - hop + dims.members) % dims.members
    query_id = pos_ref[seq, member * dims.blocks + query_slot]
    key_id = pos_ref[seq, owner * dims.blocks + key_slot]
    return jnp.logical_and(key_id < query_id, mask_ref[seq, query_id, key_id] == 1)


def causal_logits(dims, logits):
    key_token = lax.broadcasted_iota(jnp.int32, logits.shape, 0)
    query_token = lax.broadcasted_iota(jnp.int32, logits.shape, 1) // dims.heads
    return jnp.where(key_token <= query_token, logits, MASKED)


def stats_of(logits, dprob):
    parts = by_sublane(logits)
    top = jnp.max(parts, axis=0)
    exps = jnp.exp2(parts - top[None])
    return top, jnp.sum(exps, axis=0), jnp.sum(exps * by_sublane(dprob), axis=0)


def merged(first, second):
    top = jnp.maximum(first[0], second[0])
    one, two = jnp.exp2(first[0] - top), jnp.exp2(second[0] - top)
    return top, first[1] * one + second[1] * two, first[2] * one + second[2] * two


def load_stats(ref, slot):
    return ref[slot, 0], ref[slot, 1], ref[slot, 2]


def store_stats(ref, slot, stats):
    for index in range(3):
        ref[slot, index] = stats[index]


def rows_of(ref, slot, count):
    return ref[pl.ds(pl.multiple_of(slot * count, count), count), :]


def own_stats_kernel(dims, pos_ref, mask_ref, q_ref, g_ref, k_ref, v_ref, stats_ref):
    factor = dims.scale * LOG2E

    @pl.loop(0, dims.blocks)
    def _(slot):
        query = rows_of(q_ref, slot, dims.rows)
        grad = rows_of(g_ref, slot, dims.rows)

        def tile(key_slot, mask):
            logits = dot_nt(rows_of(k_ref, key_slot, BLK), query) * factor
            if mask:
                logits = causal_logits(dims, logits)
            return stats_of(logits, dot_nt(rows_of(v_ref, key_slot, BLK), grad))

        store_stats(stats_ref, slot, tile(slot, True))

        @pl.loop(0, dims.blocks)
        def _(key_slot):
            @pl.when(seen(dims, pos_ref, mask_ref, slot, 0, key_slot))
            def _():
                store_stats(stats_ref, slot, merged(load_stats(stats_ref, slot), tile(key_slot, False)))


def far_kernel(
    dims, pos_ref, mask_ref, q_ref, g_ref, near_ref, swap_ref, stats_ref,
    final_ref, dq_ref, keep_ref, send_ref,
    k_all, v_all, kt_all, run, logit_all, dprob_all, dk_all, dv_all,
):
    factor = dims.scale * LOG2E
    first_core = lax.axis_index("head") % 2 == 0
    far_blocks = (dims.members - 1) * dims.blocks

    @pl.when(first_core)
    def _():
        k_all[...] = near_ref[...]
        v_all[...] = swap_ref[...]

    @pl.when(jnp.logical_not(first_core))
    def _():
        k_all[...] = swap_ref[...]
        v_all[...] = near_ref[...]

    for index in range(far_blocks):
        kt_all[index] = k_all[index * BLK:(index + 1) * BLK, :].T

    dk_all[...] = jnp.zeros_like(dk_all)
    dv_all[...] = jnp.zeros_like(dv_all)
    run[...] = stats_ref[...]

    @pl.loop(0, dims.blocks)
    def _(slot):
        dq_ref[slot] = jnp.zeros(dq_ref.shape[1:], jnp.float32)

        def visible(index):
            return seen(dims, pos_ref, mask_ref, slot, index // dims.blocks + 1, index % dims.blocks)

        @pl.loop(0, far_blocks)
        def _(index):
            @pl.when(visible(index))
            def _():
                logits = dot_nt(rows_of(k_all, index, BLK), rows_of(q_ref, slot, dims.rows)) * factor
                dprob = dot_nt(rows_of(v_all, index, BLK), rows_of(g_ref, slot, dims.rows))
                logit_all[index] = logits
                dprob_all[index] = dprob
                store_stats(run, slot, merged(load_stats(run, slot), stats_of(logits, dprob)))

        tops, totals, weighted = load_stats(run, slot)
        top = jnp.max(tops, axis=0, keepdims=True)
        factors = jnp.exp2(tops - top)
        total = jnp.sum(totals * factors, axis=0, keepdims=True)
        log_sum = top + jnp.log2(total)
        delta = jnp.sum(weighted * factors, axis=0, keepdims=True) / total
        final_ref[slot, 0] = jnp.broadcast_to(log_sum, tops.shape)
        final_ref[slot, 1] = jnp.broadcast_to(delta, tops.shape)

        @pl.loop(0, far_blocks)
        def _(index):
            @pl.when(visible(index))
            def _():
                probs = jnp.exp2(by_sublane(logit_all[index]) - final_ref[slot, 0][None])
                dscore = probs * (by_sublane(dprob_all[index]) - final_ref[slot, 1][None])
                probs = probs.reshape(BLK, dims.rows).astype(jnp.bfloat16)
                dscore = dscore.reshape(BLK, dims.rows).astype(jnp.bfloat16)
                dk_all[index] += dot_nn(dscore, rows_of(q_ref, slot, dims.rows))
                dv_all[index] += dot_nn(probs, rows_of(g_ref, slot, dims.rows))
                dq_ref[slot] += dot_nn(kt_all[index], dscore)

    share_out(dims, first_core, dk_all, dv_all, keep_ref, send_ref)


def share_out(dims, first_core, dk_all, dv_all, keep_ref, send_ref):
    shape = keep_ref.shape

    @pl.when(first_core)
    def _():
        keep_ref[...] = (dk_all[...] * dims.scale).reshape(shape)
        send_ref[...] = dv_all[...].reshape(shape).astype(send_ref.dtype)

    @pl.when(jnp.logical_not(first_core))
    def _():
        keep_ref[...] = dv_all[...].reshape(shape)
        send_ref[...] = (dk_all[...] * dims.scale).reshape(shape).astype(send_ref.dtype)


def own_grads_kernel(
    dims, pos_ref, mask_ref, q_ref, g_ref, k_ref, v_ref, final_ref, dq_far_ref,
    dq_ref, keep_ref, send_ref,
    kt_all, dq_sum, dk_all, dv_all,
):
    factor = dims.scale * LOG2E
    first_core = lax.axis_index("head") % 2 == 0
    for index in range(dims.blocks):
        kt_all[index] = k_ref[index * BLK:(index + 1) * BLK, :].T
    dk_all[...] = jnp.zeros_like(dk_all)
    dv_all[...] = jnp.zeros_like(dv_all)

    @pl.loop(0, dims.blocks)
    def _(slot):
        query = rows_of(q_ref, slot, dims.rows)
        grad = rows_of(g_ref, slot, dims.rows)

        def tile(key_slot, mask):
            logits = dot_nt(rows_of(k_ref, key_slot, BLK), query) * factor
            if mask:
                logits = causal_logits(dims, logits)
            dprob = dot_nt(rows_of(v_ref, key_slot, BLK), grad)
            probs = jnp.exp2(by_sublane(logits) - final_ref[slot, 0][None])
            dscore = probs * (by_sublane(dprob) - final_ref[slot, 1][None])
            probs = probs.reshape(BLK, dims.rows).astype(jnp.bfloat16)
            dscore = dscore.reshape(BLK, dims.rows).astype(jnp.bfloat16)
            dk_all[key_slot] += dot_nn(dscore, query)
            dv_all[key_slot] += dot_nn(probs, grad)
            return dot_nn(kt_all[key_slot], dscore)

        dq_sum[...] = dq_far_ref[slot] + tile(slot, True)

        @pl.loop(0, dims.blocks)
        def _(key_slot):
            @pl.when(seen(dims, pos_ref, mask_ref, slot, 0, key_slot))
            def _():
                dq_sum[...] += tile(key_slot, False)

        start = pl.multiple_of(slot * dims.rows, dims.rows)
        dq_ref[pl.ds(start, dims.rows), :] = (dq_sum[...] * dims.scale).T.astype(dq_ref.dtype)

    share_out(dims, first_core, dk_all, dv_all, keep_ref, send_ref)


VMEM = pl.BlockSpec(memory_space=pltpu.VMEM)
SMEM = pl.BlockSpec(memory_space=pltpu.SMEM)


def per_device(queries, keys, values, d_out, block_pos, block_mask):
    tokens, heads, depth = queries.shape
    kv_count = keys.shape[1]
    members = lax.axis_size("ctx") // SEQS
    head_count = lax.axis_size("head")
    sharers = GROUP // heads
    dims = Shape(tokens, heads, depth, members)
    head_index = lax.axis_index("head")
    kv_index = head_index // sharers
    first_core = head_index % 2 == 0
    f32, bf16 = jnp.float32, jnp.bfloat16
    sds = jax.ShapeDtypeStruct

    key_own = lax.dynamic_index_in_dim(keys, kv_index, 1, keepdims=False) if kv_count > 1 else keys[:, 0]
    value_own = lax.dynamic_index_in_dim(values, kv_index, 1, keepdims=False) if kv_count > 1 else values[:, 0]
    query_rows = queries.reshape(tokens * heads, depth)
    grad_rows = d_out.reshape(tokens * heads, depth)

    passed = jnp.where(first_core, key_own, value_own)
    near, swap = [], []
    for _ in range(members - 1):
        passed = shifted(passed, "ctx", SEQS)
        near.append(passed)
        swap.append(swapped(passed, "head", 1))
    near = near[0] if members == 2 else jnp.concatenate(near)
    swap = swap[0] if members == 2 else jnp.concatenate(swap)

    params = pltpu.CompilerParams(vmem_limit_bytes=(12 + 4 * members) << 20)
    blocks, rows = dims.blocks, dims.rows
    tile_flops = 2 * BLK * rows * depth

    def cost(tiles, dots):
        return pl.CostEstimate(
            flops=tiles * dots * tile_flops,
            bytes_accessed=4 * tokens * heads * depth,
            transcendentals=tiles * BLK * rows,
        )

    stats = pl.pallas_call(
        functools.partial(own_stats_kernel, dims),
        out_shape=sds((blocks, 3, SUB, rows), f32),
        in_specs=[SMEM] * 2 + [VMEM] * 4,
        out_specs=VMEM,
        compiler_params=params,
        cost_estimate=cost(blocks * blocks, 2),
        name="own_stats",
    )(block_pos, block_mask, query_rows, grad_rows, key_own, value_own)

    far = (members - 1) * blocks
    final, dq_far, keep_far, send_far = pl.pallas_call(
        functools.partial(far_kernel, dims),
        out_shape=(
            sds((blocks, 2, SUB, rows), f32),
            sds((blocks, depth, rows), f32),
            sds(((members - 1) * tokens, depth), f32),
            sds(((members - 1) * tokens, depth), bf16),
        ),
        in_specs=[SMEM] * 2 + [VMEM] * 5,
        out_specs=(VMEM,) * 4,
        scratch_shapes=[
            pltpu.VMEM((far * BLK, depth), bf16),
            pltpu.VMEM((far * BLK, depth), bf16),
            pltpu.VMEM((far, depth, BLK), bf16),
            pltpu.VMEM((blocks, 3, SUB, rows), f32),
            pltpu.VMEM((far, BLK, rows), f32),
            pltpu.VMEM((far, BLK, rows), f32),
            pltpu.VMEM((far, BLK, depth), f32),
            pltpu.VMEM((far, BLK, depth), f32),
        ],
        compiler_params=params,
        cost_estimate=cost(blocks * far, 5),
        name="far_part",
    )(block_pos, block_mask, query_rows, grad_rows, near, swap, stats)

    dq, keep_own, send_own = pl.pallas_call(
        functools.partial(own_grads_kernel, dims),
        out_shape=(
            sds((tokens * heads, depth), bf16),
            sds((tokens, depth), f32),
            sds((tokens, depth), bf16),
        ),
        in_specs=[SMEM] * 2 + [VMEM] * 6,
        out_specs=(VMEM,) * 3,
        scratch_shapes=[
            pltpu.VMEM((blocks, depth, BLK), bf16),
            pltpu.VMEM((depth, rows), f32),
            pltpu.VMEM((blocks, BLK, depth), f32),
            pltpu.VMEM((blocks, BLK, depth), f32),
        ],
        compiler_params=params,
        cost_estimate=cost(blocks * blocks, 5),
        name="own_grads",
    )(block_pos, block_mask, query_rows, grad_rows, key_own, value_own, final, dq_far)

    travel = bf16 if members == 2 else f32
    pair_far = keep_far + swapped(send_far, "head", 1).astype(f32)
    total = pair_far[:tokens]
    for hop in range(1, members):
        moved = shifted(total.astype(travel), "ctx", SEQS).astype(f32)
        if hop < members - 1:
            total = moved + pair_far[hop * tokens:(hop + 1) * tokens]
    total = moved + (keep_own + swapped(send_own, "head", 1).astype(f32))
    bit = 2
    total = total.astype(bf16)
    while bit < sharers:
        total = (total.astype(f32) + swapped(total, "head", bit).astype(f32)).astype(bf16)
        bit *= 2
    other = swapped(total, "head", 1)
    d_keys = jnp.where(first_core, total, other)
    d_values = jnp.where(first_core, other, total)
    if kv_count > 1:
        groups = [[p + sharers * g for g in range(kv_count)] for p in range(sharers)]
        both = lax.all_gather(
            jnp.stack([d_keys, d_values]), "head", axis=2, axis_index_groups=groups
        )
        d_keys, d_values = both[0], both[1]
    else:
        d_keys, d_values = d_keys[:, None], d_values[:, None]
    return dq.reshape(tokens, heads, depth), d_keys, d_values


def solution(mesh):
    placed = (
        P("ctx", "head", None),
        P("ctx", None, None),
        P("ctx", None, None),
        P("ctx", "head", None),
        P(),
        P(),
    )
    return jax.shard_map(
        per_device,
        mesh=mesh,
        in_specs=placed,
        out_specs=(P("ctx", "head", None), P("ctx", None, None), P("ctx", None, None)),
        check_vma=False,
    )
```

```python
import functools

import jax
import jax.numpy as jnp
from jax import lax
from jax.experimental import pallas as pl
from jax.experimental.pallas import tpu as pltpu
from jax.sharding import PartitionSpec as P


GROUP = 16
BLK = 128
SEQS = 4
LOG2E = 1.4426950408889634
MASKED = -1e30
SUB = 8


def dot_nt(left, right):
    return lax.dot_general(
        left, right, (((1,), (1,)), ((), ())), preferred_element_type=jnp.float32
    )


def dot_nn(left, right):
    return lax.dot_general(
        left, right, (((1,), (0,)), ((), ())), preferred_element_type=jnp.float32
    )


def by_sublane(value):
    return value.reshape(value.shape[0] // SUB, SUB, value.shape[1])


def shifted(value, axis, steps):
    count = lax.axis_size(axis)
    return lax.ppermute(value, axis, [(i, (i + steps) % count) for i in range(count)])


def swapped(value, axis, bit):
    count = lax.axis_size(axis)
    return lax.ppermute(value, axis, [(i, i ^ bit) for i in range(count)])


class Shape:
    def __init__(self, tokens, heads, depth, members):
        self.heads = heads
        self.members = members
        self.blocks = tokens // BLK
        self.rows = BLK * heads
        self.scale = depth**-0.5


def place():
    ctx = lax.axis_index("ctx")
    return ctx % SEQS, ctx // SEQS


def seen(dims, pos_ref, mask_ref, query_slot, hop, key_slot):
    seq, member = place()
    owner = (member - hop + dims.members) % dims.members
    query_id = pos_ref[seq, member * dims.blocks + query_slot]
    key_id = pos_ref[seq, owner * dims.blocks + key_slot]
    return jnp.logical_and(key_id < query_id, mask_ref[seq, query_id, key_id] == 1)


def causal_logits(dims, logits):
    key_token = lax.broadcasted_iota(jnp.int32, logits.shape, 0)
    query_token = lax.broadcasted_iota(jnp.int32, logits.shape, 1) // dims.heads
    return jnp.where(key_token <= query_token, logits, MASKED)


def stats_of(logits, dprob):
    parts = by_sublane(logits)
    top = jnp.max(parts, axis=0)
    exps = jnp.exp2(parts - top[None])
    return top, jnp.sum(exps, axis=0), jnp.sum(exps * by_sublane(dprob), axis=0)


def merged(first, second):
    top = jnp.maximum(first[0], second[0])
    one, two = jnp.exp2(first[0] - top), jnp.exp2(second[0] - top)
    return top, first[1] * one + second[1] * two, first[2] * one + second[2] * two


def load_stats(ref, slot):
    return ref[slot, 0], ref[slot, 1], ref[slot, 2]


def store_stats(ref, slot, stats):
    for index in range(3):
        ref[slot, index] = stats[index]


def rows_of(ref, slot, count):
    return ref[pl.ds(pl.multiple_of(slot * count, count), count), :]


def own_stats_kernel(dims, pos_ref, mask_ref, q_ref, g_ref, k_ref, v_ref, stats_ref):
    factor = dims.scale * LOG2E

    @pl.loop(0, dims.blocks)
    def _(slot):
        query = rows_of(q_ref, slot, dims.rows)
        grad = rows_of(g_ref, slot, dims.rows)

        def tile(key_slot, mask):
            logits = dot_nt(rows_of(k_ref, key_slot, BLK), query) * factor
            if mask:
                logits = causal_logits(dims, logits)
            return stats_of(logits, dot_nt(rows_of(v_ref, key_slot, BLK), grad))

        store_stats(stats_ref, slot, tile(slot, True))

        @pl.loop(0, dims.blocks)
        def _(key_slot):
            @pl.when(seen(dims, pos_ref, mask_ref, slot, 0, key_slot))
            def _():
                store_stats(stats_ref, slot, merged(load_stats(stats_ref, slot), tile(key_slot, False)))


def far_kernel(
    dims, pos_ref, mask_ref, q_ref, g_ref, near_ref, swap_ref, stats_ref,
    final_ref, dq_ref, keep_ref, send_ref,
    k_all, v_all, kt_all, run, logit_all, dprob_all, dk_all, dv_all,
):
    factor = dims.scale * LOG2E
    first_core = lax.axis_index("head") % 2 == 0
    far_blocks = (dims.members - 1) * dims.blocks

    @pl.when(first_core)
    def _():
        k_all[...] = near_ref[...]
        v_all[...] = swap_ref[...]

    @pl.when(jnp.logical_not(first_core))
    def _():
        k_all[...] = swap_ref[...]
        v_all[...] = near_ref[...]

    for index in range(far_blocks):
        kt_all[index] = k_all[index * BLK:(index + 1) * BLK, :].T

    dk_all[...] = jnp.zeros_like(dk_all)
    dv_all[...] = jnp.zeros_like(dv_all)
    run[...] = stats_ref[...]

    @pl.loop(0, dims.blocks)
    def _(slot):
        dq_ref[slot] = jnp.zeros(dq_ref.shape[1:], jnp.float32)

        def visible(index):
            return seen(dims, pos_ref, mask_ref, slot, index // dims.blocks + 1, index % dims.blocks)

        @pl.loop(0, far_blocks)
        def _(index):
            @pl.when(visible(index))
            def _():
                logits = dot_nt(rows_of(k_all, index, BLK), rows_of(q_ref, slot, dims.rows)) * factor
                dprob = dot_nt(rows_of(v_all, index, BLK), rows_of(g_ref, slot, dims.rows))
                logit_all[index] = logits
                dprob_all[index] = dprob
                store_stats(run, slot, merged(load_stats(run, slot), stats_of(logits, dprob)))

        tops, totals, weighted = load_stats(run, slot)
        top = jnp.max(tops, axis=0, keepdims=True)
        factors = jnp.exp2(tops - top)
        total = jnp.sum(totals * factors, axis=0, keepdims=True)
        log_sum = top + jnp.log2(total)
        delta = jnp.sum(weighted * factors, axis=0, keepdims=True) / total
        final_ref[slot, 0] = jnp.broadcast_to(log_sum, tops.shape)
        final_ref[slot, 1] = jnp.broadcast_to(delta, tops.shape)

        @pl.loop(0, far_blocks)
        def _(index):
            @pl.when(visible(index))
            def _():
                probs = jnp.exp2(by_sublane(logit_all[index]) - final_ref[slot, 0][None])
                dscore = probs * (by_sublane(dprob_all[index]) - final_ref[slot, 1][None])
                probs = probs.reshape(BLK, dims.rows).astype(jnp.bfloat16)
                dscore = dscore.reshape(BLK, dims.rows).astype(jnp.bfloat16)
                dk_all[index] += dot_nn(dscore, rows_of(q_ref, slot, dims.rows))
                dv_all[index] += dot_nn(probs, rows_of(g_ref, slot, dims.rows))
                dq_ref[slot] += dot_nn(kt_all[index], dscore)

    share_out(dims, first_core, dk_all, dv_all, keep_ref, send_ref)


def share_out(dims, first_core, dk_all, dv_all, keep_ref, send_ref):
    shape = keep_ref.shape

    @pl.when(first_core)
    def _():
        keep_ref[...] = (dk_all[...] * dims.scale).reshape(shape)
        send_ref[...] = dv_all[...].reshape(shape).astype(send_ref.dtype)

    @pl.when(jnp.logical_not(first_core))
    def _():
        keep_ref[...] = dv_all[...].reshape(shape)
        send_ref[...] = (dk_all[...] * dims.scale).reshape(shape).astype(send_ref.dtype)


def own_grads_kernel(
    dims, pos_ref, mask_ref, q_ref, g_ref, k_ref, v_ref, final_ref, dq_far_ref,
    dq_ref, keep_ref, send_ref,
    kt_all, dq_sum, dk_all, dv_all,
):
    factor = dims.scale * LOG2E
    first_core = lax.axis_index("head") % 2 == 0
    for index in range(dims.blocks):
        kt_all[index] = k_ref[index * BLK:(index + 1) * BLK, :].T
    dk_all[...] = jnp.zeros_like(dk_all)
    dv_all[...] = jnp.zeros_like(dv_all)

    @pl.loop(0, dims.blocks)
    def _(slot):
        query = rows_of(q_ref, slot, dims.rows)
        grad = rows_of(g_ref, slot, dims.rows)

        def tile(key_slot, mask):
            logits = dot_nt(rows_of(k_ref, key_slot, BLK), query) * factor
            if mask:
                logits = causal_logits(dims, logits)
            dprob = dot_nt(rows_of(v_ref, key_slot, BLK), grad)
            probs = jnp.exp2(by_sublane(logits) - final_ref[slot, 0][None])
            dscore = probs * (by_sublane(dprob) - final_ref[slot, 1][None])
            probs = probs.reshape(BLK, dims.rows).astype(jnp.bfloat16)
            dscore = dscore.reshape(BLK, dims.rows).astype(jnp.bfloat16)
            dk_all[key_slot] += dot_nn(dscore, query)
            dv_all[key_slot] += dot_nn(probs, grad)
            return dot_nn(kt_all[key_slot], dscore)

        dq_sum[...] = dq_far_ref[slot] + tile(slot, True)

        @pl.loop(0, dims.blocks)
        def _(key_slot):
            @pl.when(seen(dims, pos_ref, mask_ref, slot, 0, key_slot))
            def _():
                dq_sum[...] += tile(key_slot, False)

        start = pl.multiple_of(slot * dims.rows, dims.rows)
        dq_ref[pl.ds(start, dims.rows), :] = (dq_sum[...] * dims.scale).T.astype(dq_ref.dtype)

    share_out(dims, first_core, dk_all, dv_all, keep_ref, send_ref)


VMEM = pl.BlockSpec(memory_space=pltpu.VMEM)
SMEM = pl.BlockSpec(memory_space=pltpu.SMEM)


def per_device(queries, keys, values, d_out, block_pos, block_mask):
    tokens, heads, depth = queries.shape
    kv_count = keys.shape[1]
    members = lax.axis_size("ctx") // SEQS
    sharers = GROUP // heads
    dims = Shape(tokens, heads, depth, members)
    head_index = lax.axis_index("head")
    kv_index = head_index // sharers
    first_core = head_index % 2 == 0
    f32, bf16 = jnp.float32, jnp.bfloat16
    sds = jax.ShapeDtypeStruct

    key_own = lax.dynamic_index_in_dim(keys, kv_index, 1, keepdims=False) if kv_count > 1 else keys[:, 0]
    value_own = lax.dynamic_index_in_dim(values, kv_index, 1, keepdims=False) if kv_count > 1 else values[:, 0]
    query_rows = queries.reshape(tokens * heads, depth)
    grad_rows = d_out.reshape(tokens * heads, depth)

    passed = jnp.where(first_core, key_own, value_own)
    near, swap = [], []
    for _ in range(members - 1):
        passed = shifted(passed, "ctx", SEQS)
        near.append(passed)
        swap.append(swapped(passed, "head", 1))
    near = near[0] if members == 2 else jnp.concatenate(near)
    swap = swap[0] if members == 2 else jnp.concatenate(swap)

    params = pltpu.CompilerParams(vmem_limit_bytes=(12 + 4 * members) << 20)
    blocks, rows = dims.blocks, dims.rows
    tile_flops = 2 * BLK * rows * depth

    def cost(tiles, dots):
        return pl.CostEstimate(
            flops=tiles * dots * tile_flops,
            bytes_accessed=4 * tokens * heads * depth,
            transcendentals=tiles * BLK * rows,
        )

    stats = pl.pallas_call(
        functools.partial(own_stats_kernel, dims),
        out_shape=sds((blocks, 3, SUB, rows), f32),
        in_specs=[SMEM] * 2 + [VMEM] * 4,
        out_specs=VMEM,
        compiler_params=params,
        cost_estimate=cost(blocks * blocks, 2),
        name="own_stats",
    )(block_pos, block_mask, query_rows, grad_rows, key_own, value_own)

    far = (members - 1) * blocks
    final, dq_far, keep_far, send_far = pl.pallas_call(
        functools.partial(far_kernel, dims),
        out_shape=(
            sds((blocks, 2, SUB, rows), f32),
            sds((blocks, depth, rows), f32),
            sds(((members - 1) * tokens, depth), f32),
            sds(((members - 1) * tokens, depth), bf16),
        ),
        in_specs=[SMEM] * 2 + [VMEM] * 5,
        out_specs=(VMEM,) * 4,
        scratch_shapes=[
            pltpu.VMEM((far * BLK, depth), bf16),
            pltpu.VMEM((far * BLK, depth), bf16),
            pltpu.VMEM((far, depth, BLK), bf16),
            pltpu.VMEM((blocks, 3, SUB, rows), f32),
            pltpu.VMEM((far, BLK, rows), f32),
            pltpu.VMEM((far, BLK, rows), f32),
            pltpu.VMEM((far, BLK, depth), f32),
            pltpu.VMEM((far, BLK, depth), f32),
        ],
        compiler_params=params,
        cost_estimate=cost(blocks * far, 5),
        name="far_part",
    )(block_pos, block_mask, query_rows, grad_rows, near, swap, stats)

    dq, keep_own, send_own = pl.pallas_call(
        functools.partial(own_grads_kernel, dims),
        out_shape=(
            sds((tokens * heads, depth), bf16),
            sds((tokens, depth), f32),
            sds((tokens, depth), bf16),
        ),
        in_specs=[SMEM] * 2 + [VMEM] * 6,
        out_specs=(VMEM,) * 3,
        scratch_shapes=[
            pltpu.VMEM((blocks, depth, BLK), bf16),
            pltpu.VMEM((depth, rows), f32),
            pltpu.VMEM((blocks, BLK, depth), f32),
            pltpu.VMEM((blocks, BLK, depth), f32),
        ],
        compiler_params=params,
        cost_estimate=cost(blocks * blocks, 5),
        name="own_grads",
    )(block_pos, block_mask, query_rows, grad_rows, key_own, value_own, final, dq_far)

    travel = bf16 if members == 2 else f32
    pair_far = keep_far + swapped(send_far, "head", 1).astype(f32)
    total = pair_far[:tokens]
    for hop in range(1, members):
        moved = shifted(total.astype(travel), "ctx", SEQS)
        moved = moved.astype(f32)
        if hop < members - 1:
            total = moved + pair_far[hop * tokens:(hop + 1) * tokens]
    total = moved + (keep_own + swapped(send_own, "head", 1).astype(f32))
    bit = 2
    total = total.astype(bf16)
    while bit < sharers:
        total = (total.astype(f32) + swapped(total, "head", bit).astype(f32)).astype(bf16)
        bit *= 2
    other = swapped(total, "head", 1)
    d_keys = jnp.where(first_core, total, other)
    d_values = jnp.where(first_core, other, total)
    if kv_count > 1:
        groups = [[p + sharers * g for g in range(kv_count)] for p in range(sharers)]
        both = lax.all_gather(
            jnp.stack([d_keys, d_values]), "head", axis=2, axis_index_groups=groups
        )
        d_keys, d_values = both[0], both[1]
    else:
        d_keys, d_values = d_keys[:, None], d_values[:, None]
    return dq.reshape(tokens, heads, depth), d_keys, d_values


def solution(mesh):
    placed = (
        P("ctx", "head", None),
        P("ctx", None, None),
        P("ctx", None, None),
        P("ctx", "head", None),
        P(),
        P(),
    )
    return jax.shard_map(
        per_device,
        mesh=mesh,
        in_specs=placed,
        out_specs=(P("ctx", "head", None), P("ctx", None, None), P("ctx", None, None)),
        check_vma=False,
    )
```

```python
import functools

import jax
import jax.numpy as jnp
from jax import lax
from jax.experimental import pallas as pl
from jax.experimental.pallas import tpu as pltpu
from jax.sharding import PartitionSpec as P


GROUP = 16
BLK = 128
SEQS = 4
LOG2E = 1.4426950408889634
MASKED = -1e30
SUB = 8


def dot_nt(left, right):
    return lax.dot_general(
        left, right, (((1,), (1,)), ((), ())), preferred_element_type=jnp.float32
    )


def dot_nn(left, right):
    return lax.dot_general(
        left, right, (((1,), (0,)), ((), ())), preferred_element_type=jnp.float32
    )


def by_sublane(value):
    return value.reshape(value.shape[0] // SUB, SUB, value.shape[1])


def shifted(value, axis, steps):
    count = lax.axis_size(axis)
    return lax.ppermute(value, axis, [(i, (i + steps) % count) for i in range(count)])


def swapped(value, axis, bit):
    count = lax.axis_size(axis)
    return lax.ppermute(value, axis, [(i, i ^ bit) for i in range(count)])


class Shape:
    def __init__(self, tokens, heads, depth, members):
        self.heads = heads
        self.members = members
        self.blocks = tokens // BLK
        self.far = (members - 1) * self.blocks
        self.rows = BLK * heads
        self.scale = depth**-0.5
        self.keep_tiles = self.blocks * self.far <= 32


FAR_Q, FAR_K, OWN_Q, OWN_K, COUNTS = range(5)
PLAN = (8, 128)


def causal_logits(dims, logits):
    key_token = lax.broadcasted_iota(jnp.int32, logits.shape, 0)
    query_token = lax.broadcasted_iota(jnp.int32, logits.shape, 1) // dims.heads
    return jnp.where(key_token <= query_token, logits, MASKED)


def stats_of(logits, dprob):
    parts = by_sublane(logits)
    top = jnp.max(parts, axis=0)
    exps = jnp.exp2(parts - top[None])
    return top, jnp.sum(exps, axis=0), jnp.sum(exps * by_sublane(dprob), axis=0)


def merged(first, second):
    top = jnp.maximum(first[0], second[0])
    one, two = jnp.exp2(first[0] - top), jnp.exp2(second[0] - top)
    return top, first[1] * one + second[1] * two, first[2] * one + second[2] * two


def load_stats(ref, slot):
    return ref[slot, 0], ref[slot, 1], ref[slot, 2]


def store_stats(ref, slot, stats):
    for index in range(3):
        ref[slot, index] = stats[index]


def rows_of(ref, slot, count):
    return ref[pl.ds(pl.multiple_of(slot * count, count), count), :]


def build_plan(dims, pos_ref, mask_ref, plan_ref):
    ctx = lax.axis_index("ctx")
    seq, member = lax.rem(ctx, SEQS), lax.div(ctx, SEQS)
    query_ids = [pos_ref[seq, member * dims.blocks + slot] for slot in range(dims.blocks)]

    def listed(row_q, row_k, row_count, hops):
        total = jnp.int32(0)
        for hop in hops:
            owner = member - hop
            owner = jnp.where(owner < 0, owner + dims.members, owner)
            key_ids = [pos_ref[seq, owner * dims.blocks + slot] for slot in range(dims.blocks)]
            for query_slot in range(dims.blocks):
                for key_slot in range(dims.blocks):
                    if hop == 0 and key_slot == query_slot:
                        continue
                    query_id, key_id = query_ids[query_slot], key_ids[key_slot]
                    seen = jnp.logical_and(key_id < query_id, mask_ref[seq, query_id, key_id] == 1)
                    plan_ref[row_q, total] = query_slot
                    plan_ref[row_k, total] = key_slot + max(hop - 1, 0) * dims.blocks
                    total = total + seen.astype(jnp.int32)
        plan_ref[row_q, total] = dims.blocks
        plan_ref[row_k, total] = dims.blocks if row_count else dims.far
        plan_ref[COUNTS, row_count] = lax.div(total + 1, 2)

    listed(OWN_Q, OWN_K, 1, range(1))
    listed(FAR_Q, FAR_K, 0, range(1, dims.members))


def two_at_once(count, front, back):
    def trip(step, carry):
        first, second = 2 * step, 2 * step + 1
        one, two = front(first), front(second)
        back(first, one)
        back(second, two)
        return carry

    lax.fori_loop(0, count, trip, 0)


def own_stats_kernel(
    dims, pos_hbm, mask_hbm, q_hbm, g_hbm, k_hbm, v_hbm,
    stats_ref, plan_ref, q_ref, g_ref, k_ref, v_ref,
    pos_ref, mask_ref, sums, whole_sems, slot_sems,
):
    factor = dims.scale * LOG2E
    whole = [
        pltpu.make_async_copy(source, target, whole_sems.at[index])
        for index, (source, target) in enumerate(
            ((pos_hbm, pos_ref), (mask_hbm, mask_ref), (k_hbm, k_ref), (v_hbm, v_ref))
        )
    ]
    slots = [
        [
            pltpu.make_async_copy(
                source.at[pl.ds(slot * dims.rows, dims.rows)],
                target.at[pl.ds(slot * dims.rows, dims.rows)],
                slot_sems.at[index, slot],
            )
            for index, (source, target) in enumerate(((q_hbm, q_ref), (g_hbm, g_ref)))
        ]
        for slot in range(dims.blocks)
    ]
    for copy in whole:
        copy.start()
    for pair in slots:
        for copy in pair:
            copy.start()
    whole[0].wait()
    whole[1].wait()
    build_plan(dims, pos_ref, mask_ref, plan_ref)
    whole[2].wait()
    whole[3].wait()

    def tile(query_slot, key_slot, mask):
        query_slot = jnp.minimum(query_slot, dims.blocks - 1)
        key_slot = jnp.minimum(key_slot, dims.blocks - 1)
        logits = dot_nt(rows_of(k_ref, key_slot, BLK), rows_of(q_ref, query_slot, dims.rows)) * factor
        dprob = dot_nt(rows_of(v_ref, key_slot, BLK), rows_of(g_ref, query_slot, dims.rows))
        return stats_of(causal_logits(dims, logits) if mask else logits, dprob)

    for slot in range(dims.blocks):
        slots[slot][0].wait()
        slots[slot][1].wait()
        store_stats(sums, slot, tile(slot, slot, True))

    def front(pair):
        return tile(plan_ref[OWN_Q, pair], plan_ref[OWN_K, pair], False)

    def back(pair, stats):
        slot = plan_ref[OWN_Q, pair]
        store_stats(sums, slot, merged(load_stats(sums, slot), stats))

    two_at_once(plan_ref[COUNTS, 1], front, back)
    stats_ref[...] = sums[0:dims.blocks]


def far_kernel(
    dims, plan_hbm, q_ref, g_ref, near_ref, swap_ref, stats_ref,
    final_ref, ds_ref, keep_ref, send_ref,
    plan_ref, plan_sem, k_all, v_all, run, logit_all, dprob_all, dk_all, dv_all,
):
    factor = dims.scale * LOG2E
    first_core = lax.rem(lax.axis_index("head"), 2) == 0
    load_plan = pltpu.make_async_copy(plan_hbm, plan_ref, plan_sem)
    load_plan.start()

    @pl.when(first_core)
    def _():
        k_all[...] = near_ref[...]
        v_all[...] = swap_ref[...]

    @pl.when(jnp.logical_not(first_core))
    def _():
        k_all[...] = swap_ref[...]
        v_all[...] = near_ref[...]

    dk_all[...] = jnp.zeros_like(dk_all)
    dv_all[...] = jnp.zeros_like(dv_all)
    run[0:dims.blocks] = stats_ref[...]
    load_plan.wait()
    count = plan_ref[COUNTS, 0]

    def places(pair):
        query_slot, key_slot = plan_ref[FAR_Q, pair], plan_ref[FAR_K, pair]
        return jnp.minimum(query_slot, dims.blocks - 1), jnp.minimum(key_slot, dims.far - 1)

    def tile(pair):
        query_slot, key_slot = places(pair)
        logits = dot_nt(rows_of(k_all, key_slot, BLK), rows_of(q_ref, query_slot, dims.rows)) * factor
        dprob = dot_nt(rows_of(v_all, key_slot, BLK), rows_of(g_ref, query_slot, dims.rows))
        return logits, dprob

    def stats_front(pair):
        logits, dprob = tile(pair)
        if dims.keep_tiles:
            logit_all[pair] = logits
            dprob_all[pair] = dprob
        return stats_of(logits, dprob)

    def stats_back(pair, stats):
        slot = plan_ref[FAR_Q, pair]
        store_stats(run, slot, merged(load_stats(run, slot), stats))

    two_at_once(count, stats_front, stats_back)

    for slot in range(dims.blocks):
        tops, totals, weighted = load_stats(run, slot)
        top = jnp.max(tops, axis=0, keepdims=True)
        factors = jnp.exp2(tops - top)
        total = jnp.sum(totals * factors, axis=0, keepdims=True)
        log_sum = top + jnp.log2(total)
        delta = jnp.sum(weighted * factors, axis=0, keepdims=True) / total
        final_ref[slot, 0] = jnp.broadcast_to(log_sum, tops.shape)
        final_ref[slot, 1] = jnp.broadcast_to(delta, tops.shape)

    def grads_front(pair):
        query_slot, _ = places(pair)
        logits, dprob = (logit_all[pair], dprob_all[pair]) if dims.keep_tiles else tile(pair)
        return gradient_tiles(dims, logits, dprob, final_ref, query_slot)

    def grads_back(pair, tiles):
        probs, dscore = tiles
        query_slot, _ = places(pair)
        key_slot = plan_ref[FAR_K, pair]
        ds_ref[pair] = dscore
        dk_all[key_slot] += dot_nn(dscore, rows_of(q_ref, query_slot, dims.rows))
        dv_all[key_slot] += dot_nn(probs, rows_of(g_ref, query_slot, dims.rows))

    two_at_once(count, grads_front, grads_back)
    share_out(dims, dims.far, first_core, dk_all, dv_all, keep_ref, send_ref)


def gradient_tiles(dims, logits, dprob, final_ref, slot):
    probs = jnp.exp2(by_sublane(logits) - final_ref[slot, 0][None])
    dscore = probs * (by_sublane(dprob) - final_ref[slot, 1][None])
    return (
        probs.reshape(BLK, dims.rows).astype(jnp.bfloat16),
        dscore.reshape(BLK, dims.rows).astype(jnp.bfloat16),
    )


def share_out(dims, count, first_core, dk_all, dv_all, keep_ref, send_ref):
    shape = keep_ref.shape

    @pl.when(first_core)
    def _():
        keep_ref[...] = (dk_all[0:count] * dims.scale).reshape(shape)
        send_ref[...] = dv_all[0:count].reshape(shape).astype(send_ref.dtype)

    @pl.when(jnp.logical_not(first_core))
    def _():
        keep_ref[...] = dv_all[0:count].reshape(shape)
        send_ref[...] = (dk_all[0:count] * dims.scale).reshape(shape).astype(send_ref.dtype)


def own_grads_kernel(
    dims, plan_hbm, q_ref, g_ref, k_ref, v_ref, near_ref, swap_ref, final_ref, ds_ref,
    dq_ref, keep_ref, send_ref,
    plan_ref, plan_sem, kt_own, kt_far, dq_all, dk_all, dv_all,
):
    factor = dims.scale * LOG2E
    first_core = lax.rem(lax.axis_index("head"), 2) == 0
    load_plan = pltpu.make_async_copy(plan_hbm, plan_ref, plan_sem)
    load_plan.start()
    for index in range(dims.blocks):
        kt_own[index] = k_ref[index * BLK:(index + 1) * BLK, :].T

    @pl.when(first_core)
    def _():
        for index in range(dims.far):
            kt_far[index] = near_ref[index * BLK:(index + 1) * BLK, :].T

    @pl.when(jnp.logical_not(first_core))
    def _():
        for index in range(dims.far):
            kt_far[index] = swap_ref[index * BLK:(index + 1) * BLK, :].T

    def tile(query_slot, key_slot, mask):
        logits = dot_nt(rows_of(k_ref, key_slot, BLK), rows_of(q_ref, query_slot, dims.rows)) * factor
        dprob = dot_nt(rows_of(v_ref, key_slot, BLK), rows_of(g_ref, query_slot, dims.rows))
        logits = causal_logits(dims, logits) if mask else logits
        return gradient_tiles(dims, logits, dprob, final_ref, query_slot)

    for slot in range(dims.blocks):
        probs, dscore = tile(slot, slot, True)
        dk_all[slot] = dot_nn(dscore, rows_of(q_ref, slot, dims.rows))
        dv_all[slot] = dot_nn(probs, rows_of(g_ref, slot, dims.rows))
        dq_all[slot] = dot_nn(kt_own[slot], dscore)
    load_plan.wait()

    def places(pair):
        query_slot, key_slot = plan_ref[OWN_Q, pair], plan_ref[OWN_K, pair]
        return jnp.minimum(query_slot, dims.blocks - 1), jnp.minimum(key_slot, dims.blocks - 1)

    def front(pair):
        return tile(*places(pair), False)

    def back(pair, tiles):
        probs, dscore = tiles
        query_slot, key_slot = places(pair)
        dk_all[plan_ref[OWN_K, pair]] += dot_nn(dscore, rows_of(q_ref, query_slot, dims.rows))
        dv_all[plan_ref[OWN_K, pair]] += dot_nn(probs, rows_of(g_ref, query_slot, dims.rows))
        dq_all[plan_ref[OWN_Q, pair]] += dot_nn(kt_own[key_slot], dscore)

    two_at_once(plan_ref[COUNTS, 1], front, back)

    def far_front(pair):
        key_slot = jnp.minimum(plan_ref[FAR_K, pair], dims.far - 1)
        return dot_nn(kt_far[key_slot], ds_ref[pair])

    def far_back(pair, part):
        dq_all[plan_ref[FAR_Q, pair]] += part

    two_at_once(plan_ref[COUNTS, 0], far_front, far_back)

    for slot in range(dims.blocks):
        start = slot * dims.rows
        dq_ref[start:start + dims.rows, :] = (dq_all[slot] * dims.scale).T.astype(dq_ref.dtype)

    share_out(dims, dims.blocks, first_core, dk_all, dv_all, keep_ref, send_ref)


VMEM = pl.BlockSpec(memory_space=pltpu.VMEM)
SMEM = pl.BlockSpec(memory_space=pltpu.SMEM)
HBM = pl.BlockSpec(memory_space=pltpu.HBM)


def per_device(queries, keys, values, d_out, block_pos, block_mask):
    tokens, heads, depth = queries.shape
    kv_count = keys.shape[1]
    members = lax.axis_size("ctx") // SEQS
    sharers = GROUP // heads
    dims = Shape(tokens, heads, depth, members)
    head_index = lax.axis_index("head")
    kv_index = head_index // sharers
    first_core = head_index % 2 == 0
    f32, bf16 = jnp.float32, jnp.bfloat16
    sds = jax.ShapeDtypeStruct

    key_own = lax.dynamic_index_in_dim(keys, kv_index, 1, keepdims=False) if kv_count > 1 else keys[:, 0]
    value_own = lax.dynamic_index_in_dim(values, kv_index, 1, keepdims=False) if kv_count > 1 else values[:, 0]
    query_rows = queries.reshape(tokens * heads, depth)
    grad_rows = d_out.reshape(tokens * heads, depth)

    passed = jnp.where(first_core, key_own, value_own)
    near, swap = [], []
    for _ in range(members - 1):
        passed = shifted(passed, "ctx", SEQS)
        near.append(passed)
        swap.append(swapped(passed, "head", 1))
    near = near[0] if members == 2 else jnp.concatenate(near)
    swap = swap[0] if members == 2 else jnp.concatenate(swap)

    params = pltpu.CompilerParams(vmem_limit_bytes=16 << 20)
    blocks, rows = dims.blocks, dims.rows
    tile_flops = 2 * BLK * rows * depth

    def cost(tiles, dots):
        return pl.CostEstimate(
            flops=tiles * dots * tile_flops,
            bytes_accessed=4 * tokens * heads * depth,
            transcendentals=tiles * BLK * rows,
        )

    stats, plan, query_rows, grad_rows, key_own, value_own = pl.pallas_call(
        functools.partial(own_stats_kernel, dims),
        out_shape=(
            sds((blocks, 3, SUB, rows), f32),
            sds(PLAN, jnp.int32),
            sds((tokens * heads, depth), bf16),
            sds((tokens * heads, depth), bf16),
            sds((tokens, depth), bf16),
            sds((tokens, depth), bf16),
        ),
        in_specs=[HBM] * 6,
        out_specs=(VMEM, SMEM) + (VMEM,) * 4,
        scratch_shapes=[
            pltpu.SMEM(block_pos.shape, jnp.int32),
            pltpu.SMEM(block_mask.shape, jnp.int32),
            pltpu.VMEM((blocks + 1, 3, SUB, rows), f32),
            pltpu.SemaphoreType.DMA((4,)),
            pltpu.SemaphoreType.DMA((2, blocks)),
        ],
        compiler_params=params,
        cost_estimate=cost(blocks * blocks, 2),
        name="own_stats",
    )(
        *(
            pltpu.with_memory_space_constraint(operand, pltpu.HBM)
            for operand in (block_pos, block_mask, query_rows, grad_rows, key_own, value_own)
        )
    )

    far = dims.far
    pairs = blocks * far + 2
    kept = pairs if dims.keep_tiles else 1
    final, far_scores, keep_far, send_far = pl.pallas_call(
        functools.partial(far_kernel, dims),
        out_shape=(
            sds((blocks, 2, SUB, rows), f32),
            sds((pairs, BLK, rows), bf16),
            sds((far * BLK, depth), f32),
            sds((far * BLK, depth), bf16),
        ),
        in_specs=[VMEM] * 6,
        out_specs=(VMEM,) * 4,
        scratch_shapes=[
            pltpu.SMEM(PLAN, jnp.int32),
            pltpu.SemaphoreType.DMA,
            pltpu.VMEM((far * BLK, depth), bf16),
            pltpu.VMEM((far * BLK, depth), bf16),
            pltpu.VMEM((blocks + 1, 3, SUB, rows), f32),
            pltpu.VMEM((kept, BLK, rows), f32),
            pltpu.VMEM((kept, BLK, rows), f32),
            pltpu.VMEM((far + 1, BLK, depth), f32),
            pltpu.VMEM((far + 1, BLK, depth), f32),
        ],
        compiler_params=params,
        cost_estimate=cost(blocks * far, 4),
        name="far_part",
    )(plan, query_rows, grad_rows, near, swap, stats)

    dq, keep_own, send_own = pl.pallas_call(
        functools.partial(own_grads_kernel, dims),
        out_shape=(
            sds((tokens * heads, depth), bf16),
            sds((tokens, depth), f32),
            sds((tokens, depth), bf16),
        ),
        in_specs=[VMEM] * 9,
        out_specs=(VMEM,) * 3,
        scratch_shapes=[
            pltpu.SMEM(PLAN, jnp.int32),
            pltpu.SemaphoreType.DMA,
            pltpu.VMEM((blocks, depth, BLK), bf16),
            pltpu.VMEM((far, depth, BLK), bf16),
            pltpu.VMEM((blocks + 1, depth, rows), f32),
            pltpu.VMEM((blocks + 1, BLK, depth), f32),
            pltpu.VMEM((blocks + 1, BLK, depth), f32),
        ],
        compiler_params=params,
        cost_estimate=cost(blocks * (blocks + far), 5),
        name="own_grads",
    )(plan, query_rows, grad_rows, key_own, value_own, near, swap, final, far_scores)

    travel = bf16 if members == 2 else f32
    pair_far = keep_far + swapped(send_far, "head", 1).astype(f32)
    total = pair_far[:tokens]
    for hop in range(1, members):
        moved = shifted(total.astype(travel), "ctx", SEQS)
        moved = moved.astype(f32)
        if hop < members - 1:
            total = moved + pair_far[hop * tokens:(hop + 1) * tokens]
    total = moved + (keep_own + swapped(send_own, "head", 1).astype(f32))
    bit = 2
    total = total.astype(bf16)
    while bit < sharers:
        total = (total.astype(f32) + swapped(total, "head", bit).astype(f32)).astype(bf16)
        bit *= 2
    other = swapped(total, "head", 1)
    d_keys = jnp.where(first_core, total, other)
    d_values = jnp.where(first_core, other, total)
    if kv_count > 1:
        groups = [[p + sharers * g for g in range(kv_count)] for p in range(sharers)]
        both = lax.all_gather(
            jnp.stack([d_keys, d_values]), "head", axis=2, axis_index_groups=groups
        )
        d_keys, d_values = both[0], both[1]
    else:
        d_keys, d_values = d_keys[:, None], d_values[:, None]
    return dq.reshape(tokens, heads, depth), d_keys, d_values


def solution(mesh):
    placed = (
        P("ctx", "head", None),
        P("ctx", None, None),
        P("ctx", None, None),
        P("ctx", "head", None),
        P(),
        P(),
    )
    return jax.shard_map(
        per_device,
        mesh=mesh,
        in_specs=placed,
        out_specs=(P("ctx", "head", None), P("ctx", None, None), P("ctx", None, None)),
        check_vma=False,
    )
```

```python
import functools

import jax
import jax.numpy as jnp
from jax import lax
from jax.experimental import pallas as pl
from jax.experimental.pallas import tpu as pltpu
from jax.sharding import PartitionSpec as P


GROUP = 16
BLK = 128
SEQS = 4
LOG2E = 1.4426950408889634
MASKED = -1e30
SUB = 8
PIECE = 128
PIECES = 2


def dot_nt(left, right):
    return lax.dot_general(
        left, right, (((1,), (1,)), ((), ())), preferred_element_type=jnp.float32
    )


def dot_nn(left, right):
    return lax.dot_general(
        left, right, (((1,), (0,)), ((), ())), preferred_element_type=jnp.float32
    )


def by_sublane(value):
    return value.reshape(value.shape[0] // SUB, SUB, value.shape[1])


def shifted(value, axis, steps):
    count = lax.axis_size(axis)
    return lax.ppermute(value, axis, [(i, (i + steps) % count) for i in range(count)])


def swapped(value, axis, bit):
    count = lax.axis_size(axis)
    return lax.ppermute(value, axis, [(i, i ^ bit) for i in range(count)])


class Shape:
    def __init__(self, tokens, heads, depth, members):
        self.heads = heads
        self.members = members
        self.blocks = tokens // BLK
        self.far = (members - 1) * self.blocks
        self.rows = BLK * heads
        self.scale = depth**-0.5
        self.keep_tiles = self.blocks * self.far <= 32


FAR_Q, FAR_K, OWN_Q, OWN_K, COUNTS = range(5)
PLAN = (8, 128)


def causal_logits(dims, logits):
    key_token = lax.broadcasted_iota(jnp.int32, logits.shape, 0)
    query_token = lax.broadcasted_iota(jnp.int32, logits.shape, 1) // dims.heads
    return jnp.where(key_token <= query_token, logits, MASKED)


def stats_of(logits, dprob, factor):
    parts = by_sublane(logits)
    top = jnp.max(parts, axis=0)
    exps = jnp.exp2((parts - top[None]) * factor)
    return top * factor, jnp.sum(exps, axis=0), jnp.sum(exps * by_sublane(dprob), axis=0)


def merged(first, second):
    top = jnp.maximum(first[0], second[0])
    one, two = jnp.exp2(first[0] - top), jnp.exp2(second[0] - top)
    return top, first[1] * one + second[1] * two, first[2] * one + second[2] * two


def load_stats(ref, slot):
    return ref[slot, 0], ref[slot, 1], ref[slot, 2]


def store_stats(ref, slot, stats):
    for index in range(3):
        ref[slot, index] = stats[index]


def rows_of(ref, slot, count):
    return ref[pl.ds(pl.multiple_of(slot * count, count), count), :]


def build_plan(dims, pos_ref, mask_ref, plan_ref):
    ctx = lax.axis_index("ctx")
    seq, member = lax.rem(ctx, SEQS), lax.div(ctx, SEQS)
    query_ids = [pos_ref[seq, member * dims.blocks + slot] for slot in range(dims.blocks)]

    def append(rows, total, query_slot, key_slot, seen):
        plan_ref[rows[0], total] = query_slot
        plan_ref[rows[1], total] = key_slot
        return total + jnp.asarray(seen).astype(jnp.int32)

    def sees(query_slot, key_id):
        query_id = query_ids[query_slot]
        return jnp.logical_and(key_id < query_id, mask_ref[seq, query_id, key_id] == 1)

    own = jnp.int32(0)
    for query_slot in range(dims.blocks):
        for key_slot in range(dims.blocks):
            if key_slot != query_slot:
                own = append((OWN_Q, OWN_K), own, query_slot, key_slot, sees(query_slot, query_ids[key_slot]))
    append((OWN_Q, OWN_K), own, dims.blocks, dims.blocks, True)
    plan_ref[COUNTS, 1] = lax.div(own + 1, 2)

    owners = [member - hop for hop in range(1, dims.members)]
    owners = [jnp.where(owner < 0, owner + dims.members, owner) for owner in owners]
    far_ids = [pos_ref[seq, owner * dims.blocks + slot] for owner in owners for slot in range(dims.blocks)]
    far = jnp.int32(0)
    for query_slot in range(dims.blocks):
        for key_slot, key_id in enumerate(far_ids):
            far = append((FAR_Q, FAR_K), far, query_slot, key_slot, sees(query_slot, key_id))
        far = append((FAR_Q, FAR_K), far, dims.blocks, dims.far, lax.rem(far, 2) == 1)
    plan_ref[COUNTS, 0] = lax.div(far, 2)


def two_at_once(count, front, back):
    def trip(step, carry):
        first, second = 2 * step, 2 * step + 1
        one, two = front(first), front(second)
        back(first, one)
        back(second, two)
        return carry

    lax.fori_loop(0, count, trip, 0)


def doubled(count, trips):
    def both(index, carry):
        trips((2 * index, 2 * index + 1))
        return carry

    lax.fori_loop(0, lax.div(count, 2), both, 0)

    @pl.when(lax.rem(count, 2) == 1)
    def _():
        trips((count - 1,))


def own_stats_kernel(
    dims, pos_hbm, mask_hbm, q_hbm, g_hbm, k_hbm, v_hbm,
    stats_ref, plan_ref, q_ref, g_ref, k_ref, v_ref, qt_ref, gt_ref,
    logit_ref, dprob_ref,
    pos_ref, mask_ref, sums, whole_sems, slot_sems,
):
    factor = dims.scale * LOG2E
    whole = [
        pltpu.make_async_copy(source, target, whole_sems.at[index])
        for index, (source, target) in enumerate(
            ((pos_hbm, pos_ref), (mask_hbm, mask_ref), (k_hbm, k_ref), (v_hbm, v_ref))
        )
    ]
    slots = [
        [
            pltpu.make_async_copy(
                source.at[pl.ds(slot * dims.rows, dims.rows)],
                target.at[pl.ds(slot * dims.rows, dims.rows)],
                slot_sems.at[index, slot],
            )
            for index, (source, target) in enumerate(((q_hbm, q_ref), (g_hbm, g_ref)))
        ]
        for slot in range(dims.blocks)
    ]
    for copy in whole:
        copy.start()
    for pair in slots:
        for copy in pair:
            copy.start()
    whole[0].wait()
    whole[1].wait()
    build_plan(dims, pos_ref, mask_ref, plan_ref)
    whole[2].wait()
    whole[3].wait()

    def tile(index, query_slot, key_slot, mask):
        query_slot = jnp.minimum(query_slot, dims.blocks - 1)
        key_slot = jnp.minimum(key_slot, dims.blocks - 1)
        logits = dot_nt(rows_of(k_ref, key_slot, BLK), rows_of(q_ref, query_slot, dims.rows))
        dprob = dot_nt(rows_of(v_ref, key_slot, BLK), rows_of(g_ref, query_slot, dims.rows))
        logits = causal_logits(dims, logits) if mask else logits
        logit_ref[index], dprob_ref[index] = logits, dprob
        return stats_of(logits, dprob, factor)

    for slot in range(dims.blocks):
        slots[slot][0].wait()
        slots[slot][1].wait()
        qt_ref[slot] = rows_of(q_ref, slot, dims.rows).T
        gt_ref[slot] = rows_of(g_ref, slot, dims.rows).T
        store_stats(sums, slot, tile(slot, slot, slot, True))

    def front(pair):
        return tile(dims.blocks + pair, plan_ref[OWN_Q, pair], plan_ref[OWN_K, pair], False)

    def back(pair, stats):
        slot = plan_ref[OWN_Q, pair]
        store_stats(sums, slot, merged(load_stats(sums, slot), stats))

    two_at_once(plan_ref[COUNTS, 1], front, back)
    stats_ref[...] = sums[0:dims.blocks]


def far_kernel(
    dims, plan_hbm, q_ref, g_ref, qt_ref, gt_ref, near_ref, swap_ref, stats_ref,
    final_ref, ds_ref, keep_ref, send_ref,
    plan_ref, plan_sem, k_all, v_all, run, logit_all, dprob_all, dk_all, dv_all,
):
    factor = dims.scale * LOG2E
    first_core = lax.rem(lax.axis_index("head"), 2) == 0
    load_plan = pltpu.make_async_copy(plan_hbm, plan_ref, plan_sem)
    load_plan.start()

    @pl.when(first_core)
    def _():
        k_all[...] = near_ref[...]
        v_all[...] = swap_ref[...]

    @pl.when(jnp.logical_not(first_core))
    def _():
        k_all[...] = swap_ref[...]
        v_all[...] = near_ref[...]

    dk_all[...] = jnp.zeros_like(dk_all)
    dv_all[...] = jnp.zeros_like(dv_all)
    run[0:dims.blocks] = stats_ref[...]
    load_plan.wait()
    count = plan_ref[COUNTS, 0]

    def kept(step):
        return step if dims.keep_tiles else 0

    def query_of(step):
        return jnp.minimum(plan_ref[FAR_Q, 2 * step], dims.blocks - 1)

    def pair_rows(ref, step):
        return jnp.concatenate(
            [
                rows_of(ref, jnp.minimum(plan_ref[FAR_K, 2 * step + index], dims.far - 1), BLK)
                for index in range(2)
            ]
        )

    def products(step):
        slot = query_of(step)
        logit_all[kept(step)] = dot_nn(pair_rows(k_all, step), qt_ref[slot])
        dprob_all[kept(step)] = dot_nn(pair_rows(v_all, step), gt_ref[slot])

    def statistics(step):
        return [
            stats_of(
                logit_all[kept(step), index * BLK:(index + 1) * BLK],
                dprob_all[kept(step), index * BLK:(index + 1) * BLK],
                factor,
            )
            for index in range(2)
        ]

    def merge(step, halves):
        for index in range(2):
            slot = plan_ref[FAR_Q, 2 * step + index]
            store_stats(run, slot, merged(load_stats(run, slot), halves[index]))

    def stats_trips(steps):
        halves = []
        for step in steps:
            products(step)
            halves.append(statistics(step))
        for step, half in zip(steps, halves):
            merge(step, half)

    doubled(count, stats_trips)

    for slot in range(dims.blocks):
        tops, totals, weighted = load_stats(run, slot)
        top = jnp.max(tops, axis=0, keepdims=True)
        factors = jnp.exp2(tops - top)
        total = jnp.sum(totals * factors, axis=0, keepdims=True)
        log_sum = top + jnp.log2(total)
        delta = jnp.sum(weighted * factors, axis=0, keepdims=True) / total
        final_ref[slot, 0] = jnp.broadcast_to(log_sum, tops.shape)
        final_ref[slot, 1] = jnp.broadcast_to(delta, tops.shape)

    def gradients(step):
        slot = query_of(step)
        if not dims.keep_tiles:
            products(step)
        dk_part, dv_part = 0.0, 0.0
        for piece in range(dims.rows // PIECE):
            part = slice(piece * PIECE, (piece + 1) * PIECE)
            probs, dscore = gradient_tiles(
                logit_all[kept(step), :, part], dprob_all[kept(step), :, part], final_ref, slot, part, factor
            )
            ds_ref[step, :, part] = dscore
            dk_part += dot_nn(dscore, piece_of(dims, q_ref, slot, piece))
            dv_part += dot_nn(probs, piece_of(dims, g_ref, slot, piece))
        return dk_part, dv_part

    def grads_trips(steps):
        sums = [gradients(step) for step in steps]
        for step, (dk_part, dv_part) in zip(steps, sums):
            for index in range(2):
                key_slot = plan_ref[FAR_K, 2 * step + index]
                dk_all[key_slot] += dk_part[index * BLK:(index + 1) * BLK]
                dv_all[key_slot] += dv_part[index * BLK:(index + 1) * BLK]

    doubled(count, grads_trips)
    share_out(dims, dims.far, first_core, dk_all, dv_all, keep_ref, send_ref)


def piece_of(dims, ref, slot, piece):
    return ref[pl.ds(pl.multiple_of(slot * dims.rows + piece * PIECE, PIECE), PIECE), :]


def gradient_tiles(logits, dprob, final_ref, slot, part, factor):
    probs = jnp.exp2(by_sublane(logits) * factor - final_ref[slot, 0, :, part][None])
    dscore = probs * (by_sublane(dprob) - final_ref[slot, 1, :, part][None])
    return (
        probs.reshape(logits.shape).astype(jnp.bfloat16),
        dscore.reshape(logits.shape).astype(jnp.bfloat16),
    )


def share_out(dims, count, first_core, dk_all, dv_all, keep_ref, send_ref):
    shape = keep_ref.shape

    @pl.when(first_core)
    def _():
        keep_ref[...] = (dk_all[0:count] * dims.scale).reshape(shape)
        send_ref[...] = dv_all[0:count].reshape(shape).astype(send_ref.dtype)

    @pl.when(jnp.logical_not(first_core))
    def _():
        keep_ref[...] = dv_all[0:count].reshape(shape)
        send_ref[...] = (dk_all[0:count] * dims.scale).reshape(shape).astype(send_ref.dtype)


def own_sums_kernel(
    dims, plan_hbm, q_ref, g_ref, final_ref, logit_ref, dprob_ref,
    keep_ref, send_ref, ds_ref,
    plan_ref, plan_sem, dk_all, dv_all,
):
    factor = dims.scale * LOG2E
    first_core = lax.rem(lax.axis_index("head"), 2) == 0
    load_plan = pltpu.make_async_copy(plan_hbm, plan_ref, plan_sem)
    load_plan.start()

    def front(index, query_slot):
        probs, dscore = gradient_tiles(
            logit_ref[index], dprob_ref[index], final_ref, query_slot, slice(None), factor
        )
        ds_ref[index] = dscore
        return (
            dot_nn(dscore, rows_of(q_ref, query_slot, dims.rows)),
            dot_nn(probs, rows_of(g_ref, query_slot, dims.rows)),
        )

    for slot in range(dims.blocks):
        dk_all[slot], dv_all[slot] = front(slot, slot)
    load_plan.wait()

    def own_front(pair):
        return front(dims.blocks + pair, jnp.minimum(plan_ref[OWN_Q, pair], dims.blocks - 1))

    def own_back(pair, sums):
        dk_all[plan_ref[OWN_K, pair]] += sums[0]
        dv_all[plan_ref[OWN_K, pair]] += sums[1]

    two_at_once(plan_ref[COUNTS, 1], own_front, own_back)
    share_out(dims, dims.blocks, first_core, dk_all, dv_all, keep_ref, send_ref)


def queries_kernel(
    dims, plan_hbm, k_ref, near_ref, swap_ref, far_ds_ref, own_ds_ref,
    dq_ref,
    plan_ref, plan_sem, kt_own, kt_far, dq_all,
):
    first_core = lax.rem(lax.axis_index("head"), 2) == 0
    load_plan = pltpu.make_async_copy(plan_hbm, plan_ref, plan_sem)
    load_plan.start()
    for index in range(dims.blocks):
        kt_own[index] = k_ref[index * BLK:(index + 1) * BLK, :].T

    @pl.when(first_core)
    def _():
        for index in range(dims.far):
            kt_far[index] = near_ref[index * BLK:(index + 1) * BLK, :].T

    @pl.when(jnp.logical_not(first_core))
    def _():
        for index in range(dims.far):
            kt_far[index] = swap_ref[index * BLK:(index + 1) * BLK, :].T

    for slot in range(dims.blocks):
        dq_all[slot] = dot_nn(kt_own[slot], own_ds_ref[slot])
    load_plan.wait()

    def own_front(pair):
        key_slot = jnp.minimum(plan_ref[OWN_K, pair], dims.blocks - 1)
        return dot_nn(kt_own[key_slot], own_ds_ref[dims.blocks + pair])

    def own_back(pair, part):
        dq_all[plan_ref[OWN_Q, pair]] += part

    two_at_once(plan_ref[COUNTS, 1], own_front, own_back)

    def far_trip(step, carry):
        slot = jnp.minimum(plan_ref[FAR_Q, 2 * step], dims.blocks - 1)
        parts = [
            dot_nn(
                kt_far[jnp.minimum(plan_ref[FAR_K, 2 * step + index], dims.far - 1)],
                far_ds_ref[step, index * BLK:(index + 1) * BLK],
            )
            for index in range(2)
        ]
        real = plan_ref[FAR_Q, 2 * step + 1] < dims.blocks
        dq_all[slot] += parts[0] + jnp.where(real, parts[1], 0.0)
        return carry

    lax.fori_loop(0, plan_ref[COUNTS, 0], far_trip, 0)

    for slot in range(dims.blocks):
        start = slot * dims.rows
        dq_ref[start:start + dims.rows, :] = (dq_all[slot] * dims.scale).T.astype(dq_ref.dtype)


def pick_kernel(k_hbm, v_hbm, out_ref):
    first_core = lax.rem(lax.axis_index("head"), 2) == 0

    @pl.when(first_core)
    def _():
        pltpu.sync_copy(k_hbm, out_ref)

    @pl.when(jnp.logical_not(first_core))
    def _():
        pltpu.sync_copy(v_hbm, out_ref)


def place_kernel(*refs):
    own_refs, other_refs, (dk_hbm, dv_hbm, sems) = refs[:PIECES], refs[PIECES:2 * PIECES], refs[2 * PIECES:]
    first_core = lax.rem(lax.axis_index("head"), 2) == 0
    starts = [sum(ref.shape[0] for ref in own_refs[:index]) for index in range(PIECES)]

    def put(dk_refs, dv_refs):
        copies = [
            pltpu.make_async_copy(ref, target.at[pl.ds(starts[index], ref.shape[0])], sems.at[which, index])
            for which, (sources, target) in enumerate(((dk_refs, dk_hbm), (dv_refs, dv_hbm)))
            for index, ref in enumerate(sources)
        ]
        for copy in copies:
            copy.start()
        for copy in copies:
            copy.wait()

    @pl.when(first_core)
    def _():
        put(own_refs, other_refs)

    @pl.when(jnp.logical_not(first_core))
    def _():
        put(other_refs, own_refs)


VMEM = pl.BlockSpec(memory_space=pltpu.VMEM)
SMEM = pl.BlockSpec(memory_space=pltpu.SMEM)
HBM = pl.BlockSpec(memory_space=pltpu.HBM)


def per_device(queries, keys, values, d_out, block_pos, block_mask):
    tokens, heads, depth = queries.shape
    kv_count = keys.shape[1]
    members = lax.axis_size("ctx") // SEQS
    sharers = GROUP // heads
    dims = Shape(tokens, heads, depth, members)
    head_index = lax.axis_index("head")
    kv_index = head_index // sharers
    f32, bf16 = jnp.float32, jnp.bfloat16
    sds = jax.ShapeDtypeStruct

    key_own = lax.dynamic_index_in_dim(keys, kv_index, 1, keepdims=False) if kv_count > 1 else keys[:, 0]
    value_own = lax.dynamic_index_in_dim(values, kv_index, 1, keepdims=False) if kv_count > 1 else values[:, 0]
    query_rows = queries.reshape(tokens * heads, depth)
    grad_rows = d_out.reshape(tokens * heads, depth)

    passed = pl.pallas_call(
        pick_kernel,
        out_shape=sds((tokens, depth), bf16),
        in_specs=[HBM] * 2,
        out_specs=VMEM,
        compiler_params=pltpu.CompilerParams(vmem_limit_bytes=1 << 20),
        name="pick",
    )(*(pltpu.with_memory_space_constraint(operand, pltpu.HBM) for operand in (key_own, value_own)))
    near, swap = [], []
    for _ in range(members - 1):
        passed = shifted(passed, "ctx", SEQS)
        near.append(passed)
        swap.append(swapped(passed, "head", 1))
    near = near[0] if members == 2 else jnp.concatenate(near)
    swap = swap[0] if members == 2 else jnp.concatenate(swap)

    params = pltpu.CompilerParams(vmem_limit_bytes=16 << 20)
    blocks, rows = dims.blocks, dims.rows
    tile_flops = 2 * BLK * rows * depth

    def cost(tiles, dots):
        return pl.CostEstimate(
            flops=tiles * dots * tile_flops,
            bytes_accessed=4 * tokens * heads * depth,
            transcendentals=tiles * BLK * rows,
        )

    own_pairs = blocks + blocks * (blocks - 1) // 2 + 1
    (
        stats, plan, query_rows, grad_rows, key_own, value_own, query_cols, grad_cols, own_logits, own_dprobs,
    ) = pl.pallas_call(
        functools.partial(own_stats_kernel, dims),
        out_shape=(
            sds((blocks, 3, SUB, rows), f32),
            sds(PLAN, jnp.int32),
            sds((tokens * heads, depth), bf16),
            sds((tokens * heads, depth), bf16),
            sds((tokens, depth), bf16),
            sds((tokens, depth), bf16),
            sds((blocks, depth, rows), bf16),
            sds((blocks, depth, rows), bf16),
            sds((own_pairs, BLK, rows), f32),
            sds((own_pairs, BLK, rows), f32),
        ),
        in_specs=[HBM] * 6,
        out_specs=(VMEM, SMEM) + (VMEM,) * 8,
        scratch_shapes=[
            pltpu.SMEM(block_pos.shape, jnp.int32),
            pltpu.SMEM(block_mask.shape, jnp.int32),
            pltpu.VMEM((blocks + 1, 3, SUB, rows), f32),
            pltpu.SemaphoreType.DMA((4,)),
            pltpu.SemaphoreType.DMA((2, blocks)),
        ],
        compiler_params=params,
        cost_estimate=cost(blocks * blocks, 2),
        name="own_stats",
    )(
        *(
            pltpu.with_memory_space_constraint(operand, pltpu.HBM)
            for operand in (block_pos, block_mask, query_rows, grad_rows, key_own, value_own)
        )
    )

    far = dims.far
    trips = blocks * pl.cdiv(far, 2)
    kept = trips if dims.keep_tiles else 1
    final, far_scores, keep_far, send_far = pl.pallas_call(
        functools.partial(far_kernel, dims),
        out_shape=(
            sds((blocks, 2, SUB, rows), f32),
            sds((trips, 2 * BLK, rows), bf16),
            sds((far * BLK, depth), f32),
            sds((far * BLK, depth), bf16),
        ),
        in_specs=[VMEM] * 8,
        out_specs=(VMEM,) * 4,
        scratch_shapes=[
            pltpu.SMEM(PLAN, jnp.int32),
            pltpu.SemaphoreType.DMA,
            pltpu.VMEM((far * BLK, depth), bf16),
            pltpu.VMEM((far * BLK, depth), bf16),
            pltpu.VMEM((blocks + 1, 3, SUB, rows), f32),
            pltpu.VMEM((kept, 2 * BLK, rows), f32),
            pltpu.VMEM((kept, 2 * BLK, rows), f32),
            pltpu.VMEM((far + 1, BLK, depth), f32),
            pltpu.VMEM((far + 1, BLK, depth), f32),
        ],
        compiler_params=params,
        cost_estimate=cost(blocks * far, 4),
        name="far_part",
    )(plan, query_rows, grad_rows, query_cols, grad_cols, near, swap, stats)

    keep_own, send_own, own_scores = pl.pallas_call(
        functools.partial(own_sums_kernel, dims),
        out_shape=(
            sds((tokens, depth), f32),
            sds((tokens, depth), bf16),
            sds((own_pairs, BLK, rows), bf16),
        ),
        in_specs=[VMEM] * 6,
        out_specs=(VMEM,) * 3,
        scratch_shapes=[
            pltpu.SMEM(PLAN, jnp.int32),
            pltpu.SemaphoreType.DMA,
            pltpu.VMEM((blocks + 1, BLK, depth), f32),
            pltpu.VMEM((blocks + 1, BLK, depth), f32),
        ],
        compiler_params=params,
        cost_estimate=cost(blocks * blocks, 2),
        name="own_sums",
    )(plan, query_rows, grad_rows, final, own_logits, own_dprobs)

    dq = pl.pallas_call(
        functools.partial(queries_kernel, dims),
        out_shape=sds((tokens * heads, depth), bf16),
        in_specs=[VMEM] * 6,
        out_specs=VMEM,
        scratch_shapes=[
            pltpu.SMEM(PLAN, jnp.int32),
            pltpu.SemaphoreType.DMA,
            pltpu.VMEM((blocks, depth, BLK), bf16),
            pltpu.VMEM((far, depth, BLK), bf16),
            pltpu.VMEM((blocks + 1, depth, rows), f32),
        ],
        compiler_params=params,
        cost_estimate=cost(blocks * (blocks + far), 1),
        name="queries",
    )(plan, key_own, near, swap, far_scores, own_scores)

    cuts = (0, tokens // 2 + 16, tokens)
    travel = bf16 if members == 2 else f32
    pair_far = keep_far + swapped(send_far, "head", 1).astype(f32)

    def far_piece(hop, index):
        return pair_far[(hop - 1) * tokens + cuts[index]:(hop - 1) * tokens + cuts[index + 1]]

    totals = [far_piece(1, index) for index in range(PIECES)]
    for hop in range(1, members):
        for index in range(PIECES):
            totals[index] = shifted(totals[index].astype(travel), "ctx", SEQS)
            if hop < members - 1:
                totals[index] = totals[index].astype(f32) + far_piece(hop + 1, index)
    swapped_own = swapped(send_own, "head", 1)
    pair_own = keep_own + swapped_own.astype(f32)
    others = []
    for index in range(PIECES):
        total = (totals[index].astype(f32) + pair_own[cuts[index]:cuts[index + 1]]).astype(bf16)
        bit = 2
        while bit < sharers:
            moved = swapped(total, "head", bit)
            total = (total.astype(f32) + moved.astype(f32)).astype(bf16)
            bit *= 2
        totals[index] = total
        others.append(swapped(total, "head", 1))
    d_keys, d_values = pl.pallas_call(
        place_kernel,
        out_shape=(sds((tokens, depth), bf16),) * 2,
        in_specs=[VMEM] * (2 * PIECES),
        out_specs=(HBM,) * 2,
        scratch_shapes=[pltpu.SemaphoreType.DMA((2, PIECES))],
        compiler_params=pltpu.CompilerParams(vmem_limit_bytes=1 << 20),
        name="place",
    )(*totals, *others)
    if kv_count > 1:
        groups = [[p + sharers * g for g in range(kv_count)] for p in range(sharers)]
        both = lax.all_gather(
            jnp.stack([d_keys, d_values]), "head", axis=2, axis_index_groups=groups
        )
        d_keys, d_values = both[0], both[1]
    else:
        d_keys, d_values = d_keys[:, None], d_values[:, None]
    return dq.reshape(tokens, heads, depth), d_keys, d_values


def solution(mesh):
    placed = (
        P("ctx", "head", None),
        P("ctx", None, None),
        P("ctx", None, None),
        P("ctx", "head", None),
        P(),
        P(),
    )
    return jax.shard_map(
        per_device,
        mesh=mesh,
        in_specs=placed,
        out_specs=(P("ctx", "head", None), P("ctx", None, None), P("ctx", None, None)),
        check_vma=False,
    )
```

```python
import functools

import jax
import jax.numpy as jnp
from jax import lax
from jax.experimental import pallas as pl
from jax.experimental.pallas import tpu as pltpu
from jax.sharding import PartitionSpec as P


GROUP = 16
BLK = 128
SEQS = 4
LOG2E = 1.4426950408889634
MASKED = -1e30
SUB = 8
PIECE = 128
PIECES = 2
COPIES = 4


def dot_nt(left, right):
    return lax.dot_general(
        left, right, (((1,), (1,)), ((), ())), preferred_element_type=jnp.float32
    )


def dot_nn(left, right):
    return lax.dot_general(
        left, right, (((1,), (0,)), ((), ())), preferred_element_type=jnp.float32
    )


def by_sublane(value):
    return value.reshape(value.shape[0] // SUB, SUB, value.shape[1])


def shifted(value, axis, steps):
    count = lax.axis_size(axis)
    return lax.ppermute(value, axis, [(i, (i + steps) % count) for i in range(count)])


def swapped(value, axis, bit):
    count = lax.axis_size(axis)
    return lax.ppermute(value, axis, [(i, i ^ bit) for i in range(count)])


class Shape:
    def __init__(self, tokens, heads, depth, members):
        self.heads = heads
        self.members = members
        self.blocks = tokens // BLK
        self.far = (members - 1) * self.blocks
        self.rows = BLK * heads
        self.scale = depth**-0.5
        self.keep_tiles = self.blocks * self.far <= 32


FAR_Q, FAR_K, OWN_Q, OWN_K, COUNTS = range(5)
PLAN = (8, 128)


def causal_logits(dims, logits):
    key_token = lax.broadcasted_iota(jnp.int32, logits.shape, 0)
    query_token = lax.broadcasted_iota(jnp.int32, logits.shape, 1) // dims.heads
    return jnp.where(key_token <= query_token, logits, MASKED)


def stats_of(logits, dprob, factor):
    parts = by_sublane(logits)
    top = jnp.max(parts, axis=0)
    exps = jnp.exp2((parts - top[None]) * factor)
    return top * factor, jnp.sum(exps, axis=0), jnp.sum(exps * by_sublane(dprob), axis=0)


def merged(first, second):
    top = jnp.maximum(first[0], second[0])
    one, two = jnp.exp2(first[0] - top), jnp.exp2(second[0] - top)
    return top, first[1] * one + second[1] * two, first[2] * one + second[2] * two


def load_stats(ref, slot):
    return ref[slot, 0], ref[slot, 1], ref[slot, 2]


def store_stats(ref, slot, stats):
    for index in range(3):
        ref[slot, index] = stats[index]


def rows_of(ref, slot, count):
    return ref[pl.ds(pl.multiple_of(slot * count, count), count), :]


def build_plan(dims, pos_ref, mask_ref, plan_ref):
    ctx = lax.axis_index("ctx")
    seq, member = lax.rem(ctx, SEQS), lax.div(ctx, SEQS)
    query_ids = [pos_ref[seq, member * dims.blocks + slot] for slot in range(dims.blocks)]

    def append(rows, total, query_slot, key_slot, seen):
        plan_ref[rows[0], total] = query_slot
        plan_ref[rows[1], total] = key_slot
        return total + jnp.asarray(seen).astype(jnp.int32)

    def sees(query_slot, key_id):
        query_id = query_ids[query_slot]
        return jnp.logical_and(key_id < query_id, mask_ref[seq, query_id, key_id] == 1)

    own = jnp.int32(0)
    for query_slot in range(dims.blocks):
        for key_slot in range(dims.blocks):
            if key_slot != query_slot:
                own = append((OWN_Q, OWN_K), own, query_slot, key_slot, sees(query_slot, query_ids[key_slot]))
    append((OWN_Q, OWN_K), own, dims.blocks, dims.blocks, True)
    plan_ref[COUNTS, 1] = lax.div(own + 1, 2)

    owners = [member - hop for hop in range(1, dims.members)]
    owners = [jnp.where(owner < 0, owner + dims.members, owner) for owner in owners]
    far_ids = [pos_ref[seq, owner * dims.blocks + slot] for owner in owners for slot in range(dims.blocks)]
    far = jnp.int32(0)
    for query_slot in range(dims.blocks):
        for key_slot, key_id in enumerate(far_ids):
            far = append((FAR_Q, FAR_K), far, query_slot, key_slot, sees(query_slot, key_id))
        far = append((FAR_Q, FAR_K), far, dims.blocks, dims.far, lax.rem(far, 2) == 1)
    plan_ref[COUNTS, 0] = lax.div(far, 2)


def two_at_once(count, front, back):
    def trip(step, carry):
        first, second = 2 * step, 2 * step + 1
        one, two = front(first), front(second)
        back(first, one)
        back(second, two)
        return carry

    lax.fori_loop(0, count, trip, 0)


def doubled(count, trips):
    def both(index, carry):
        trips((2 * index, 2 * index + 1))
        return carry

    lax.fori_loop(0, lax.div(count, 2), both, 0)

    @pl.when(lax.rem(count, 2) == 1)
    def _():
        trips((count - 1,))


def own_stats_kernel(
    dims, pos_hbm, mask_hbm, q_hbm, g_hbm, k_hbm, v_hbm,
    stats_ref, plan_ref, q_ref, g_ref, k_ref, v_ref, qt_ref, gt_ref,
    logit_ref, dprob_ref,
    pos_ref, mask_ref, sums, whole_sems, slot_sems,
):
    factor = dims.scale * LOG2E
    whole = [
        pltpu.make_async_copy(source, target, whole_sems.at[index])
        for index, (source, target) in enumerate(
            ((pos_hbm, pos_ref), (mask_hbm, mask_ref), (k_hbm, k_ref), (v_hbm, v_ref))
        )
    ]
    slots = [
        [
            pltpu.make_async_copy(
                source.at[pl.ds(slot * dims.rows, dims.rows)],
                target.at[pl.ds(slot * dims.rows, dims.rows)],
                slot_sems.at[index, slot],
            )
            for index, (source, target) in enumerate(((q_hbm, q_ref), (g_hbm, g_ref)))
        ]
        for slot in range(dims.blocks)
    ]
    for copy in whole:
        copy.start()
    for pair in slots:
        for copy in pair:
            copy.start()
    whole[0].wait()
    whole[1].wait()
    build_plan(dims, pos_ref, mask_ref, plan_ref)
    whole[2].wait()
    whole[3].wait()

    def tile(index, query_slot, key_slot, mask):
        query_slot = jnp.minimum(query_slot, dims.blocks - 1)
        key_slot = jnp.minimum(key_slot, dims.blocks - 1)
        logits = dot_nt(rows_of(k_ref, key_slot, BLK), rows_of(q_ref, query_slot, dims.rows))
        dprob = dot_nt(rows_of(v_ref, key_slot, BLK), rows_of(g_ref, query_slot, dims.rows))
        logits = causal_logits(dims, logits) if mask else logits
        logit_ref[index], dprob_ref[index] = logits, dprob
        return stats_of(logits, dprob, factor)

    for slot in range(dims.blocks):
        slots[slot][0].wait()
        slots[slot][1].wait()
        qt_ref[slot] = rows_of(q_ref, slot, dims.rows).T
        gt_ref[slot] = rows_of(g_ref, slot, dims.rows).T
        store_stats(sums, slot, tile(slot, slot, slot, True))

    def front(pair):
        return tile(dims.blocks + pair, plan_ref[OWN_Q, pair], plan_ref[OWN_K, pair], False)

    def back(pair, stats):
        slot = plan_ref[OWN_Q, pair]
        store_stats(sums, slot, merged(load_stats(sums, slot), stats))

    two_at_once(plan_ref[COUNTS, 1], front, back)
    stats_ref[...] = sums[0:dims.blocks]


def far_kernel(
    dims, plan_hbm, q_ref, g_ref, qt_ref, gt_ref, near_ref, swap_ref, stats_ref,
    final_ref, ds_ref, keep_ref, send_ref,
    plan_ref, plan_sem, k_all, v_all, run, logit_all, dprob_all, dk_all, dv_all,
):
    factor = dims.scale * LOG2E
    first_core = lax.rem(lax.axis_index("head"), 2) == 0
    load_plan = pltpu.make_async_copy(plan_hbm, plan_ref, plan_sem)
    load_plan.start()

    @pl.when(first_core)
    def _():
        k_all[...] = near_ref[...]
        v_all[...] = swap_ref[...]

    @pl.when(jnp.logical_not(first_core))
    def _():
        k_all[...] = swap_ref[...]
        v_all[...] = near_ref[...]

    dk_all[...] = jnp.zeros_like(dk_all)
    dv_all[...] = jnp.zeros_like(dv_all)
    run[0:dims.blocks] = stats_ref[...]
    load_plan.wait()
    count = plan_ref[COUNTS, 0]

    def kept(step):
        return step if dims.keep_tiles else 0

    def query_of(step):
        return jnp.minimum(plan_ref[FAR_Q, 2 * step], dims.blocks - 1)

    def pair_rows(ref, step):
        return jnp.concatenate(
            [
                rows_of(ref, jnp.minimum(plan_ref[FAR_K, 2 * step + index], dims.far - 1), BLK)
                for index in range(2)
            ]
        )

    def products(step):
        slot = query_of(step)
        logit_all[kept(step)] = dot_nn(pair_rows(k_all, step), qt_ref[slot])
        dprob_all[kept(step)] = dot_nn(pair_rows(v_all, step), gt_ref[slot])

    def statistics(step):
        return [
            stats_of(
                logit_all[kept(step), index * BLK:(index + 1) * BLK],
                dprob_all[kept(step), index * BLK:(index + 1) * BLK],
                factor,
            )
            for index in range(2)
        ]

    def merge(step, halves):
        for index in range(2):
            slot = plan_ref[FAR_Q, 2 * step + index]
            store_stats(run, slot, merged(load_stats(run, slot), halves[index]))

    def stats_trips(steps):
        halves = []
        for step in steps:
            products(step)
            halves.append(statistics(step))
        for step, half in zip(steps, halves):
            merge(step, half)

    doubled(count, stats_trips)

    for slot in range(dims.blocks):
        tops, totals, weighted = load_stats(run, slot)
        top = jnp.max(tops, axis=0, keepdims=True)
        factors = jnp.exp2(tops - top)
        total = jnp.sum(totals * factors, axis=0, keepdims=True)
        log_sum = top + jnp.log2(total)
        delta = jnp.sum(weighted * factors, axis=0, keepdims=True) / total
        final_ref[slot, 0] = jnp.broadcast_to(log_sum, tops.shape)
        final_ref[slot, 1] = jnp.broadcast_to(delta, tops.shape)

    def gradients(step):
        slot = query_of(step)
        if not dims.keep_tiles:
            products(step)
        dk_part, dv_part = 0.0, 0.0
        for piece in range(dims.rows // PIECE):
            part = slice(piece * PIECE, (piece + 1) * PIECE)
            probs, dscore = gradient_tiles(
                logit_all[kept(step), :, part], dprob_all[kept(step), :, part], final_ref, slot, part, factor
            )
            ds_ref[step, :, part] = dscore
            dk_part += dot_nn(dscore, piece_of(dims, q_ref, slot, piece))
            dv_part += dot_nn(probs, piece_of(dims, g_ref, slot, piece))
        return dk_part, dv_part

    def grads_trips(steps):
        sums = [gradients(step) for step in steps]
        for step, (dk_part, dv_part) in zip(steps, sums):
            for index in range(2):
                key_slot = plan_ref[FAR_K, 2 * step + index]
                dk_all[key_slot] += dk_part[index * BLK:(index + 1) * BLK]
                dv_all[key_slot] += dv_part[index * BLK:(index + 1) * BLK]

    doubled(count, grads_trips)
    share_out(dims, dims.far, first_core, dk_all, dv_all, keep_ref, send_ref)


def piece_of(dims, ref, slot, piece):
    return ref[pl.ds(pl.multiple_of(slot * dims.rows + piece * PIECE, PIECE), PIECE), :]


def gradient_tiles(logits, dprob, final_ref, slot, part, factor):
    probs = jnp.exp2(by_sublane(logits) * factor - final_ref[slot, 0, :, part][None])
    dscore = probs * (by_sublane(dprob) - final_ref[slot, 1, :, part][None])
    return (
        probs.reshape(logits.shape).astype(jnp.bfloat16),
        dscore.reshape(logits.shape).astype(jnp.bfloat16),
    )


def share_out(dims, count, first_core, dk_all, dv_all, keep_ref, send_ref):
    shape = keep_ref.shape

    @pl.when(first_core)
    def _():
        keep_ref[...] = (dk_all[0:count] * dims.scale).reshape(shape)
        send_ref[...] = dv_all[0:count].reshape(shape).astype(send_ref.dtype)

    @pl.when(jnp.logical_not(first_core))
    def _():
        keep_ref[...] = dv_all[0:count].reshape(shape)
        send_ref[...] = (dk_all[0:count] * dims.scale).reshape(shape).astype(send_ref.dtype)


def own_sums_kernel(
    dims, plan_hbm, q_ref, g_ref, final_ref, logit_ref, dprob_ref,
    keep_ref, send_ref, ds_ref,
    plan_ref, plan_sem, dk_all, dv_all,
):
    factor = dims.scale * LOG2E
    first_core = lax.rem(lax.axis_index("head"), 2) == 0
    load_plan = pltpu.make_async_copy(plan_hbm, plan_ref, plan_sem)
    load_plan.start()

    def front(index, query_slot):
        probs, dscore = gradient_tiles(
            logit_ref[index], dprob_ref[index], final_ref, query_slot, slice(None), factor
        )
        ds_ref[index] = dscore
        return (
            dot_nn(dscore, rows_of(q_ref, query_slot, dims.rows)),
            dot_nn(probs, rows_of(g_ref, query_slot, dims.rows)),
        )

    for slot in range(dims.blocks):
        dk_all[slot], dv_all[slot] = front(slot, slot)
    load_plan.wait()

    def own_front(pair):
        return front(dims.blocks + pair, jnp.minimum(plan_ref[OWN_Q, pair], dims.blocks - 1))

    def own_back(pair, sums):
        dk_all[plan_ref[OWN_K, pair]] += sums[0]
        dv_all[plan_ref[OWN_K, pair]] += sums[1]

    two_at_once(plan_ref[COUNTS, 1], own_front, own_back)
    share_out(dims, dims.blocks, first_core, dk_all, dv_all, keep_ref, send_ref)


def own_queries_kernel(
    dims, plan_hbm, k_ref, near_ref, swap_ref, own_ds_ref,
    dq_ref, kt_far,
    plan_ref, plan_sem, kt_own,
):
    first_core = lax.rem(lax.axis_index("head"), 2) == 0
    load_plan = pltpu.make_async_copy(plan_hbm, plan_ref, plan_sem)
    load_plan.start()
    for index in range(dims.blocks):
        kt_own[index] = k_ref[index * BLK:(index + 1) * BLK, :].T

    @pl.when(first_core)
    def _():
        for index in range(dims.far):
            kt_far[index] = near_ref[index * BLK:(index + 1) * BLK, :].T

    @pl.when(jnp.logical_not(first_core))
    def _():
        for index in range(dims.far):
            kt_far[index] = swap_ref[index * BLK:(index + 1) * BLK, :].T

    for slot in range(dims.blocks):
        dq_ref[slot] = dot_nn(kt_own[slot], own_ds_ref[slot])
    load_plan.wait()

    def own_front(pair):
        key_slot = jnp.minimum(plan_ref[OWN_K, pair], dims.blocks - 1)
        return dot_nn(kt_own[key_slot], own_ds_ref[dims.blocks + pair])

    def own_back(pair, part):
        dq_ref[plan_ref[OWN_Q, pair]] += part

    two_at_once(plan_ref[COUNTS, 1], own_front, own_back)


def queries_kernel(
    dims, plan_hbm, kt_far, far_ds_ref, dq_own_ref,
    dq_hbm,
    plan_ref, plan_sem, dq_all, dq_out, dq_sems,
):
    load_plan = pltpu.make_async_copy(plan_hbm, plan_ref, plan_sem)
    load_plan.start()
    dq_all[...] = dq_own_ref[0:dims.blocks]
    load_plan.wait()

    def far_trip(step, carry):
        slot = jnp.minimum(plan_ref[FAR_Q, 2 * step], dims.blocks - 1)
        parts = [
            dot_nn(
                kt_far[jnp.minimum(plan_ref[FAR_K, 2 * step + index], dims.far - 1)],
                far_ds_ref[step, index * BLK:(index + 1) * BLK],
            )
            for index in range(2)
        ]
        real = plan_ref[FAR_Q, 2 * step + 1] < dims.blocks
        dq_all[slot] += parts[0] + jnp.where(real, parts[1], 0.0)
        return carry

    lax.fori_loop(0, plan_ref[COUNTS, 0], far_trip, 0)

    copies = []
    for slot in range(dims.blocks):
        part = pl.ds(slot * dims.rows, dims.rows)
        dq_out[part, :] = (dq_all[slot] * dims.scale).T.astype(dq_out.dtype)
        copies.append(pltpu.make_async_copy(dq_out.at[part], dq_hbm.at[part], dq_sems.at[slot]))
        copies[-1].start()
    for copy in copies:
        copy.wait()


def pick_kernel(k_hbm, v_hbm, out_ref, sems):
    first_core = lax.rem(lax.axis_index("head"), 2) == 0
    rows = out_ref.shape[0] // COPIES

    def take(source):
        copies = [
            pltpu.make_async_copy(
                source.at[pl.ds(index * rows, rows)], out_ref.at[pl.ds(index * rows, rows)], sems.at[index]
            )
            for index in range(COPIES)
        ]
        for copy in copies:
            copy.start()
        for copy in copies:
            copy.wait()

    @pl.when(first_core)
    def _():
        take(k_hbm)

    @pl.when(jnp.logical_not(first_core))
    def _():
        take(v_hbm)


def place_kernel(*refs):
    own_refs, other_refs, (dk_hbm, dv_hbm, sems) = refs[:PIECES], refs[PIECES:2 * PIECES], refs[2 * PIECES:]
    first_core = lax.rem(lax.axis_index("head"), 2) == 0
    starts = [sum(ref.shape[0] for ref in own_refs[:index]) for index in range(PIECES)]

    def put(dk_refs, dv_refs):
        copies = [
            pltpu.make_async_copy(ref, target.at[pl.ds(starts[index], ref.shape[0])], sems.at[which, index])
            for which, (sources, target) in enumerate(((dk_refs, dk_hbm), (dv_refs, dv_hbm)))
            for index, ref in enumerate(sources)
        ]
        for copy in copies:
            copy.start()
        for copy in copies:
            copy.wait()

    @pl.when(first_core)
    def _():
        put(own_refs, other_refs)

    @pl.when(jnp.logical_not(first_core))
    def _():
        put(other_refs, own_refs)


VMEM = pl.BlockSpec(memory_space=pltpu.VMEM)
SMEM = pl.BlockSpec(memory_space=pltpu.SMEM)
HBM = pl.BlockSpec(memory_space=pltpu.HBM)


def per_device(queries, keys, values, d_out, block_pos, block_mask):
    tokens, heads, depth = queries.shape
    kv_count = keys.shape[1]
    members = lax.axis_size("ctx") // SEQS
    sharers = GROUP // heads
    dims = Shape(tokens, heads, depth, members)
    head_index = lax.axis_index("head")
    kv_index = head_index // sharers
    f32, bf16 = jnp.float32, jnp.bfloat16
    sds = jax.ShapeDtypeStruct

    key_own = lax.dynamic_index_in_dim(keys, kv_index, 1, keepdims=False) if kv_count > 1 else keys[:, 0]
    value_own = lax.dynamic_index_in_dim(values, kv_index, 1, keepdims=False) if kv_count > 1 else values[:, 0]
    query_rows = queries.reshape(tokens * heads, depth)
    grad_rows = d_out.reshape(tokens * heads, depth)

    passed = pl.pallas_call(
        pick_kernel,
        out_shape=sds((tokens, depth), bf16),
        in_specs=[HBM] * 2,
        out_specs=VMEM,
        scratch_shapes=[pltpu.SemaphoreType.DMA((COPIES,))],
        compiler_params=pltpu.CompilerParams(vmem_limit_bytes=1 << 20),
        name="pick",
    )(*(pltpu.with_memory_space_constraint(operand, pltpu.HBM) for operand in (key_own, value_own)))
    near, swap = [], []
    for _ in range(members - 1):
        passed = shifted(passed, "ctx", SEQS)
        near.append(passed)
        swap.append(swapped(passed, "head", 1))
    near = near[0] if members == 2 else jnp.concatenate(near)
    swap = swap[0] if members == 2 else jnp.concatenate(swap)

    params = pltpu.CompilerParams(vmem_limit_bytes=16 << 20)
    blocks, rows = dims.blocks, dims.rows
    tile_flops = 2 * BLK * rows * depth

    def cost(tiles, dots):
        return pl.CostEstimate(
            flops=tiles * dots * tile_flops,
            bytes_accessed=4 * tokens * heads * depth,
            transcendentals=tiles * BLK * rows,
        )

    own_pairs = blocks + blocks * (blocks - 1) // 2 + 1
    (
        stats, plan, query_rows, grad_rows, key_own, value_own, query_cols, grad_cols, own_logits, own_dprobs,
    ) = pl.pallas_call(
        functools.partial(own_stats_kernel, dims),
        out_shape=(
            sds((blocks, 3, SUB, rows), f32),
            sds(PLAN, jnp.int32),
            sds((tokens * heads, depth), bf16),
            sds((tokens * heads, depth), bf16),
            sds((tokens, depth), bf16),
            sds((tokens, depth), bf16),
            sds((blocks, depth, rows), bf16),
            sds((blocks, depth, rows), bf16),
            sds((own_pairs, BLK, rows), f32),
            sds((own_pairs, BLK, rows), f32),
        ),
        in_specs=[HBM] * 6,
        out_specs=(VMEM, SMEM) + (VMEM,) * 8,
        scratch_shapes=[
            pltpu.SMEM(block_pos.shape, jnp.int32),
            pltpu.SMEM(block_mask.shape, jnp.int32),
            pltpu.VMEM((blocks + 1, 3, SUB, rows), f32),
            pltpu.SemaphoreType.DMA((4,)),
            pltpu.SemaphoreType.DMA((2, blocks)),
        ],
        compiler_params=params,
        cost_estimate=cost(blocks * blocks, 2),
        name="own_stats",
    )(
        *(
            pltpu.with_memory_space_constraint(operand, pltpu.HBM)
            for operand in (block_pos, block_mask, query_rows, grad_rows, key_own, value_own)
        )
    )

    far = dims.far
    trips = blocks * pl.cdiv(far, 2)
    kept = trips if dims.keep_tiles else 1
    final, far_scores, keep_far, send_far = pl.pallas_call(
        functools.partial(far_kernel, dims),
        out_shape=(
            sds((blocks, 2, SUB, rows), f32),
            sds((trips, 2 * BLK, rows), bf16),
            sds((far * BLK, depth), f32),
            sds((far * BLK, depth), bf16),
        ),
        in_specs=[VMEM] * 8,
        out_specs=(VMEM,) * 4,
        scratch_shapes=[
            pltpu.SMEM(PLAN, jnp.int32),
            pltpu.SemaphoreType.DMA,
            pltpu.VMEM((far * BLK, depth), bf16),
            pltpu.VMEM((far * BLK, depth), bf16),
            pltpu.VMEM((blocks + 1, 3, SUB, rows), f32),
            pltpu.VMEM((kept, 2 * BLK, rows), f32),
            pltpu.VMEM((kept, 2 * BLK, rows), f32),
            pltpu.VMEM((far + 1, BLK, depth), f32),
            pltpu.VMEM((far + 1, BLK, depth), f32),
        ],
        compiler_params=params,
        cost_estimate=cost(blocks * far, 4),
        name="far_part",
    )(plan, query_rows, grad_rows, query_cols, grad_cols, near, swap, stats)

    keep_own, send_own, own_scores = pl.pallas_call(
        functools.partial(own_sums_kernel, dims),
        out_shape=(
            sds((tokens, depth), f32),
            sds((tokens, depth), bf16),
            sds((own_pairs, BLK, rows), bf16),
        ),
        in_specs=[VMEM] * 6,
        out_specs=(VMEM,) * 3,
        scratch_shapes=[
            pltpu.SMEM(PLAN, jnp.int32),
            pltpu.SemaphoreType.DMA,
            pltpu.VMEM((blocks + 1, BLK, depth), f32),
            pltpu.VMEM((blocks + 1, BLK, depth), f32),
        ],
        compiler_params=params,
        cost_estimate=cost(blocks * blocks, 2),
        name="own_sums",
    )(plan, query_rows, grad_rows, final, own_logits, own_dprobs)

    dq_own, far_cols = pl.pallas_call(
        functools.partial(own_queries_kernel, dims),
        out_shape=(sds((blocks + 1, depth, rows), f32), sds((far, depth, BLK), bf16)),
        in_specs=[VMEM] * 5,
        out_specs=(VMEM,) * 2,
        scratch_shapes=[
            pltpu.SMEM(PLAN, jnp.int32),
            pltpu.SemaphoreType.DMA,
            pltpu.VMEM((blocks, depth, BLK), bf16),
        ],
        compiler_params=params,
        cost_estimate=cost(blocks * blocks, 1),
        name="own_queries",
    )(plan, key_own, near, swap, own_scores)

    dq = pl.pallas_call(
        functools.partial(queries_kernel, dims),
        out_shape=sds((tokens * heads, depth), bf16),
        in_specs=[VMEM] * 4,
        out_specs=HBM,
        scratch_shapes=[
            pltpu.SMEM(PLAN, jnp.int32),
            pltpu.SemaphoreType.DMA,
            pltpu.VMEM((blocks, depth, rows), f32),
            pltpu.VMEM((tokens * heads, depth), bf16),
            pltpu.SemaphoreType.DMA((blocks,)),
        ],
        compiler_params=params,
        cost_estimate=cost(blocks * far, 1),
        name="queries",
    )(plan, far_cols, far_scores, dq_own)

    cuts = (0, tokens * 5 // 8, tokens)
    travel = bf16 if members == 2 else f32
    pair_far = keep_far + swapped(send_far, "head", 1).astype(f32)

    def far_piece(hop, index):
        return pair_far[(hop - 1) * tokens + cuts[index]:(hop - 1) * tokens + cuts[index + 1]]

    totals = [far_piece(1, index) for index in range(PIECES)]
    for hop in range(1, members):
        for index in range(PIECES):
            totals[index] = shifted(totals[index].astype(travel), "ctx", SEQS)
            if hop < members - 1:
                totals[index] = totals[index].astype(f32) + far_piece(hop + 1, index)
    swapped_own = swapped(send_own, "head", 1)
    pair_own = keep_own + swapped_own.astype(f32)
    others = []
    for index in range(PIECES):
        total = (totals[index].astype(f32) + pair_own[cuts[index]:cuts[index + 1]]).astype(bf16)
        bit = 2
        while bit < sharers:
            moved = swapped(total, "head", bit)
            total = (total.astype(f32) + moved.astype(f32)).astype(bf16)
            bit *= 2
        totals[index] = total
        others.append(swapped(total, "head", 1))
    d_keys, d_values = pl.pallas_call(
        place_kernel,
        out_shape=(sds((tokens, depth), bf16),) * 2,
        in_specs=[VMEM] * (2 * PIECES),
        out_specs=(HBM,) * 2,
        scratch_shapes=[pltpu.SemaphoreType.DMA((2, PIECES))],
        compiler_params=pltpu.CompilerParams(vmem_limit_bytes=1 << 20),
        name="place",
    )(*totals, *others)
    if kv_count > 1:
        groups = [[p + sharers * g for g in range(kv_count)] for p in range(sharers)]
        both = lax.all_gather(
            jnp.stack([d_keys, d_values]), "head", axis=2, axis_index_groups=groups
        )
        d_keys, d_values = both[0], both[1]
    else:
        d_keys, d_values = d_keys[:, None], d_values[:, None]
    return dq.reshape(tokens, heads, depth), d_keys, d_values


def solution(mesh):
    placed = (
        P("ctx", "head", None),
        P("ctx", None, None),
        P("ctx", None, None),
        P("ctx", "head", None),
        P(),
        P(),
    )
    return jax.shard_map(
        per_device,
        mesh=mesh,
        in_specs=placed,
        out_specs=(P("ctx", "head", None), P("ctx", None, None), P("ctx", None, None)),
        check_vma=False,
    )
```

```python
import functools

import jax
import jax.numpy as jnp
from jax import lax
from jax.experimental import pallas as pl
from jax.experimental.pallas import tpu as pltpu
from jax.sharding import PartitionSpec as P


GROUP = 16
BLK = 128
SEQS = 4
LOG2E = 1.4426950408889634
MASKED = -1e30
SUB = 8
PIECE = 128
PIECES = 2
COPIES = 8


def dot_nt(left, right):
    return lax.dot_general(
        left, right, (((1,), (1,)), ((), ())), preferred_element_type=jnp.float32
    )


def dot_nn(left, right):
    return lax.dot_general(
        left, right, (((1,), (0,)), ((), ())), preferred_element_type=jnp.float32
    )


def by_sublane(value):
    return value.reshape(value.shape[0] // SUB, SUB, value.shape[1])


def shifted(value, axis, steps):
    count = lax.axis_size(axis)
    return lax.ppermute(value, axis, [(i, (i + steps) % count) for i in range(count)])


def swapped(value, axis, bit):
    count = lax.axis_size(axis)
    return lax.ppermute(value, axis, [(i, i ^ bit) for i in range(count)])


class Shape:
    def __init__(self, tokens, heads, depth, members):
        self.heads = heads
        self.members = members
        self.blocks = tokens // BLK
        self.far = (members - 1) * self.blocks
        self.rows = BLK * heads
        self.scale = depth**-0.5
        self.keep_tiles = self.blocks * self.far <= 32


FAR_Q, FAR_K, OWN_Q, OWN_K = range(4)
PLAN = (8, 128)


def causal_logits(dims, logits):
    key_token = lax.broadcasted_iota(jnp.int32, logits.shape, 0)
    query_token = lax.broadcasted_iota(jnp.int32, logits.shape, 1) // dims.heads
    return jnp.where(key_token <= query_token, logits, MASKED)


def stats_of(logits, dprob, factor):
    parts = by_sublane(logits)
    top = jnp.max(parts, axis=0)
    exps = jnp.exp2((parts - top[None]) * factor)
    return top * factor, jnp.sum(exps, axis=0), jnp.sum(exps * by_sublane(dprob), axis=0)


def merged(first, second):
    top = jnp.maximum(first[0], second[0])
    one, two = jnp.exp2(first[0] - top), jnp.exp2(second[0] - top)
    return top, first[1] * one + second[1] * two, first[2] * one + second[2] * two


def load_stats(ref, slot):
    return ref[slot, 0], ref[slot, 1], ref[slot, 2]


def store_stats(ref, slot, stats):
    for index in range(3):
        ref[slot, index] = stats[index]


def rows_of(ref, slot, count):
    return ref[pl.ds(pl.multiple_of(slot * count, count), count), :]


def seen_words(dims, pos_ref, mask_ref, bits_ref):
    ctx = lax.axis_index("ctx")
    seq, member = lax.rem(ctx, SEQS), lax.div(ctx, SEQS)
    own_ids = [pos_ref[seq, member * dims.blocks + slot] for slot in range(dims.blocks)]
    owners = [member - hop for hop in range(1, dims.members)]
    owners = [jnp.where(owner < 0, owner + dims.members, owner) for owner in owners]
    far_ids = [pos_ref[seq, owner * dims.blocks + slot] for owner in owners for slot in range(dims.blocks)]
    words = []
    for key_ids in (far_ids, own_ids):
        for query_id in own_ids:
            word = jnp.int32(0)
            for index, key_id in enumerate(key_ids):
                seen = jnp.logical_and(key_id < query_id, mask_ref[seq, query_id, key_id] == 1)
                word += jnp.where(seen, 1 << index, 0)
            words.append(word)
    for row, word in enumerate(words):
        bits_ref[row:row + 1, :] = jnp.full((1, bits_ref.shape[1]), word, jnp.int32)
    return words


def append(plan_ref, rows, total, query_slot, key_slot, seen):
    plan_ref[rows[0], total] = query_slot
    plan_ref[rows[1], total] = key_slot
    return total + jnp.asarray(seen).astype(jnp.int32)


def list_own(dims, words, plan_ref):
    total = jnp.int32(0)
    for query_slot, word in enumerate(words[dims.blocks:]):
        for key_slot in range(dims.blocks):
            if key_slot != query_slot:
                seen = lax.rem(lax.shift_right_logical(word, key_slot), 2) == 1
                total = append(plan_ref, (OWN_Q, OWN_K), total, query_slot, key_slot, seen)
    append(plan_ref, (OWN_Q, OWN_K), total, dims.blocks, dims.blocks, True)
    return lax.div(total + 1, 2)


def list_far(dims, words, plan_ref):
    total = jnp.int32(0)
    for query_slot, word in enumerate(words[:dims.blocks]):
        for key_slot in range(dims.far):
            seen = lax.rem(lax.shift_right_logical(word, key_slot), 2) == 1
            total = append(plan_ref, (FAR_Q, FAR_K), total, query_slot, key_slot, seen)
        total = append(plan_ref, (FAR_Q, FAR_K), total, dims.blocks, dims.far, lax.rem(total, 2) == 1)
    return lax.div(total, 2)


def read_words(dims, bits_ref):
    return [bits_ref[row, 0] for row in range(2 * dims.blocks)]


def two_at_once(count, front, back):
    def trip(step, carry):
        first, second = 2 * step, 2 * step + 1
        one, two = front(first), front(second)
        back(first, one)
        back(second, two)
        return carry

    lax.fori_loop(0, count, trip, 0)


def doubled(count, trips):
    def both(index, carry):
        trips((2 * index, 2 * index + 1))
        return carry

    lax.fori_loop(0, lax.div(count, 2), both, 0)

    @pl.when(lax.rem(count, 2) == 1)
    def _():
        trips((count - 1,))


def own_stats_kernel(
    dims, pos_hbm, mask_hbm, q_hbm, g_hbm, k_hbm, v_hbm,
    stats_ref, bits_ref, q_ref, g_ref, k_ref, v_ref, qt_ref, gt_ref,
    logit_ref, dprob_ref,
    plan_ref, pos_ref, mask_ref, sums, whole_sems, slot_sems,
):
    factor = dims.scale * LOG2E
    whole = [
        pltpu.make_async_copy(source, target, whole_sems.at[index])
        for index, (source, target) in enumerate(
            ((pos_hbm, pos_ref), (mask_hbm, mask_ref), (k_hbm, k_ref), (v_hbm, v_ref))
        )
    ]
    slots = [
        [
            pltpu.make_async_copy(
                source.at[pl.ds(slot * dims.rows, dims.rows)],
                target.at[pl.ds(slot * dims.rows, dims.rows)],
                slot_sems.at[index, slot],
            )
            for index, (source, target) in enumerate(((q_hbm, q_ref), (g_hbm, g_ref)))
        ]
        for slot in range(dims.blocks)
    ]
    for copy in whole:
        copy.start()
    for pair in slots:
        for copy in pair:
            copy.start()
    whole[0].wait()
    whole[1].wait()
    count = list_own(dims, seen_words(dims, pos_ref, mask_ref, bits_ref), plan_ref)
    whole[2].wait()
    whole[3].wait()

    def tile(index, query_slot, key_slot, mask):
        query_slot = jnp.minimum(query_slot, dims.blocks - 1)
        key_slot = jnp.minimum(key_slot, dims.blocks - 1)
        logits = dot_nt(rows_of(k_ref, key_slot, BLK), rows_of(q_ref, query_slot, dims.rows))
        dprob = dot_nt(rows_of(v_ref, key_slot, BLK), rows_of(g_ref, query_slot, dims.rows))
        logits = causal_logits(dims, logits) if mask else logits
        logit_ref[index], dprob_ref[index] = logits, dprob
        return stats_of(logits, dprob, factor)

    for slot in range(dims.blocks):
        slots[slot][0].wait()
        slots[slot][1].wait()
        qt_ref[slot] = rows_of(q_ref, slot, dims.rows).T
        gt_ref[slot] = rows_of(g_ref, slot, dims.rows).T
        store_stats(sums, slot, tile(slot, slot, slot, True))

    def front(pair):
        return tile(dims.blocks + pair, plan_ref[OWN_Q, pair], plan_ref[OWN_K, pair], False)

    def back(pair, stats):
        slot = plan_ref[OWN_Q, pair]
        store_stats(sums, slot, merged(load_stats(sums, slot), stats))

    two_at_once(count, front, back)
    stats_ref[...] = sums[0:dims.blocks]


def far_kernel(
    dims, bits_ref, q_ref, g_ref, qt_ref, gt_ref, near_ref, swap_ref, stats_ref,
    final_ref, ds_ref, keep_ref, send_ref,
    plan_ref, k_all, v_all, run, logit_all, dprob_all, dk_all, dv_all,
):
    factor = dims.scale * LOG2E
    first_core = lax.rem(lax.axis_index("head"), 2) == 0
    words = read_words(dims, bits_ref)

    @pl.when(first_core)
    def _():
        k_all[...] = near_ref[...]
        v_all[...] = swap_ref[...]

    @pl.when(jnp.logical_not(first_core))
    def _():
        k_all[...] = swap_ref[...]
        v_all[...] = near_ref[...]

    dk_all[...] = jnp.zeros_like(dk_all)
    dv_all[...] = jnp.zeros_like(dv_all)
    run[0:dims.blocks] = stats_ref[...]
    count = list_far(dims, words, plan_ref)

    def kept(step):
        return step if dims.keep_tiles else 0

    def query_of(step):
        return jnp.minimum(plan_ref[FAR_Q, 2 * step], dims.blocks - 1)

    def pair_rows(ref, step):
        return jnp.concatenate(
            [
                rows_of(ref, jnp.minimum(plan_ref[FAR_K, 2 * step + index], dims.far - 1), BLK)
                for index in range(2)
            ]
        )

    def products(step):
        slot = query_of(step)
        logit_all[kept(step)] = dot_nn(pair_rows(k_all, step), qt_ref[slot])
        dprob_all[kept(step)] = dot_nn(pair_rows(v_all, step), gt_ref[slot])

    def statistics(step):
        return [
            stats_of(
                logit_all[kept(step), index * BLK:(index + 1) * BLK],
                dprob_all[kept(step), index * BLK:(index + 1) * BLK],
                factor,
            )
            for index in range(2)
        ]

    def merge(step, halves):
        for index in range(2):
            slot = plan_ref[FAR_Q, 2 * step + index]
            store_stats(run, slot, merged(load_stats(run, slot), halves[index]))

    def stats_trips(steps):
        halves = []
        for step in steps:
            products(step)
            halves.append(statistics(step))
        for step, half in zip(steps, halves):
            merge(step, half)

    doubled(count, stats_trips)

    for slot in range(dims.blocks):
        tops, totals, weighted = load_stats(run, slot)
        top = jnp.max(tops, axis=0, keepdims=True)
        factors = jnp.exp2(tops - top)
        total = jnp.sum(totals * factors, axis=0, keepdims=True)
        log_sum = top + jnp.log2(total)
        delta = jnp.sum(weighted * factors, axis=0, keepdims=True) / total
        final_ref[slot, 0] = jnp.broadcast_to(log_sum, tops.shape)
        final_ref[slot, 1] = jnp.broadcast_to(delta, tops.shape)

    def gradients(step):
        slot = query_of(step)
        if not dims.keep_tiles:
            products(step)
        dk_part, dv_part = 0.0, 0.0
        for piece in range(dims.rows // PIECE):
            part = slice(piece * PIECE, (piece + 1) * PIECE)
            probs, dscore = gradient_tiles(
                logit_all[kept(step), :, part], dprob_all[kept(step), :, part], final_ref, slot, part, factor
            )
            ds_ref[step, :, part] = dscore
            dk_part += dot_nn(dscore, piece_of(dims, q_ref, slot, piece))
            dv_part += dot_nn(probs, piece_of(dims, g_ref, slot, piece))
        return dk_part, dv_part

    def grads_trips(steps):
        sums = [gradients(step) for step in steps]
        for step, (dk_part, dv_part) in zip(steps, sums):
            for index in range(2):
                key_slot = plan_ref[FAR_K, 2 * step + index]
                dk_all[key_slot] += dk_part[index * BLK:(index + 1) * BLK]
                dv_all[key_slot] += dv_part[index * BLK:(index + 1) * BLK]

    doubled(count, grads_trips)
    share_out(dims, dims.far, first_core, dk_all, dv_all, keep_ref, send_ref)


def piece_of(dims, ref, slot, piece):
    return ref[pl.ds(pl.multiple_of(slot * dims.rows + piece * PIECE, PIECE), PIECE), :]


def gradient_tiles(logits, dprob, final_ref, slot, part, factor):
    probs = jnp.exp2(by_sublane(logits) * factor - final_ref[slot, 0, :, part][None])
    dscore = probs * (by_sublane(dprob) - final_ref[slot, 1, :, part][None])
    return (
        probs.reshape(logits.shape).astype(jnp.bfloat16),
        dscore.reshape(logits.shape).astype(jnp.bfloat16),
    )


def share_out(dims, count, first_core, dk_all, dv_all, keep_ref, send_ref):
    shape = keep_ref.shape

    @pl.when(first_core)
    def _():
        keep_ref[...] = (dk_all[0:count] * dims.scale).reshape(shape)
        send_ref[...] = dv_all[0:count].reshape(shape).astype(send_ref.dtype)

    @pl.when(jnp.logical_not(first_core))
    def _():
        keep_ref[...] = dv_all[0:count].reshape(shape)
        send_ref[...] = (dk_all[0:count] * dims.scale).reshape(shape).astype(send_ref.dtype)


def own_sums_kernel(
    dims, bits_ref, q_ref, g_ref, final_ref, logit_ref, dprob_ref,
    keep_ref, send_ref, ds_ref,
    plan_ref, dk_all, dv_all,
):
    factor = dims.scale * LOG2E
    first_core = lax.rem(lax.axis_index("head"), 2) == 0
    words = read_words(dims, bits_ref)

    def front(index, query_slot):
        probs, dscore = gradient_tiles(
            logit_ref[index], dprob_ref[index], final_ref, query_slot, slice(None), factor
        )
        ds_ref[index] = dscore
        return (
            dot_nn(dscore, rows_of(q_ref, query_slot, dims.rows)),
            dot_nn(probs, rows_of(g_ref, query_slot, dims.rows)),
        )

    for slot in range(dims.blocks):
        dk_all[slot], dv_all[slot] = front(slot, slot)
    count = list_own(dims, words, plan_ref)

    def own_front(pair):
        return front(dims.blocks + pair, jnp.minimum(plan_ref[OWN_Q, pair], dims.blocks - 1))

    def own_back(pair, sums):
        dk_all[plan_ref[OWN_K, pair]] += sums[0]
        dv_all[plan_ref[OWN_K, pair]] += sums[1]

    two_at_once(count, own_front, own_back)
    share_out(dims, dims.blocks, first_core, dk_all, dv_all, keep_ref, send_ref)


def own_queries_kernel(
    dims, bits_ref, k_ref, near_ref, swap_ref, own_ds_ref,
    dq_ref, kt_far,
    plan_ref, kt_own,
):
    first_core = lax.rem(lax.axis_index("head"), 2) == 0
    words = read_words(dims, bits_ref)
    for index in range(dims.blocks):
        kt_own[index] = k_ref[index * BLK:(index + 1) * BLK, :].T

    @pl.when(first_core)
    def _():
        for index in range(dims.far):
            kt_far[index] = near_ref[index * BLK:(index + 1) * BLK, :].T

    @pl.when(jnp.logical_not(first_core))
    def _():
        for index in range(dims.far):
            kt_far[index] = swap_ref[index * BLK:(index + 1) * BLK, :].T

    for slot in range(dims.blocks):
        dq_ref[slot] = dot_nn(kt_own[slot], own_ds_ref[slot])
    count = list_own(dims, words, plan_ref)

    def own_front(pair):
        key_slot = jnp.minimum(plan_ref[OWN_K, pair], dims.blocks - 1)
        return dot_nn(kt_own[key_slot], own_ds_ref[dims.blocks + pair])

    def own_back(pair, part):
        dq_ref[plan_ref[OWN_Q, pair]] += part

    two_at_once(count, own_front, own_back)


def queries_kernel(
    dims, bits_ref, kt_far, far_ds_ref, dq_own_ref,
    dq_hbm,
    plan_ref, dq_all, dq_out, dq_sems,
):
    words = read_words(dims, bits_ref)
    dq_all[...] = dq_own_ref[0:dims.blocks]
    count = list_far(dims, words, plan_ref)

    def far_trip(step, carry):
        slot = jnp.minimum(plan_ref[FAR_Q, 2 * step], dims.blocks - 1)
        parts = [
            dot_nn(
                kt_far[jnp.minimum(plan_ref[FAR_K, 2 * step + index], dims.far - 1)],
                far_ds_ref[step, index * BLK:(index + 1) * BLK],
            )
            for index in range(2)
        ]
        real = plan_ref[FAR_Q, 2 * step + 1] < dims.blocks
        dq_all[slot] += parts[0] + jnp.where(real, parts[1], 0.0)
        return carry

    lax.fori_loop(0, count, far_trip, 0)

    copies = []
    for slot in range(dims.blocks):
        part = pl.ds(slot * dims.rows, dims.rows)
        dq_out[part, :] = (dq_all[slot] * dims.scale).T.astype(dq_out.dtype)
        copies.append(pltpu.make_async_copy(dq_out.at[part], dq_hbm.at[part], dq_sems.at[slot]))
        copies[-1].start()
    for copy in copies:
        copy.wait()


def pick_kernel(k_hbm, v_hbm, out_ref, sems):
    first_core = lax.rem(lax.axis_index("head"), 2) == 0
    rows = out_ref.shape[0] // COPIES

    def take(source):
        copies = [
            pltpu.make_async_copy(
                source.at[pl.ds(index * rows, rows)], out_ref.at[pl.ds(index * rows, rows)], sems.at[index]
            )
            for index in range(COPIES)
        ]
        for copy in copies:
            copy.start()
        for copy in copies:
            copy.wait()

    @pl.when(first_core)
    def _():
        take(k_hbm)

    @pl.when(jnp.logical_not(first_core))
    def _():
        take(v_hbm)


def place_kernel(*refs):
    own_refs, other_refs, (dk_hbm, dv_hbm, sems) = refs[:PIECES], refs[PIECES:2 * PIECES], refs[2 * PIECES:]
    first_core = lax.rem(lax.axis_index("head"), 2) == 0
    starts = [sum(ref.shape[0] for ref in own_refs[:index]) for index in range(PIECES)]

    def put(dk_refs, dv_refs):
        copies = [
            pltpu.make_async_copy(ref, target.at[pl.ds(starts[index], ref.shape[0])], sems.at[which, index])
            for which, (sources, target) in enumerate(((dk_refs, dk_hbm), (dv_refs, dv_hbm)))
            for index, ref in enumerate(sources)
        ]
        for copy in copies:
            copy.start()
        for copy in copies:
            copy.wait()

    @pl.when(first_core)
    def _():
        put(own_refs, other_refs)

    @pl.when(jnp.logical_not(first_core))
    def _():
        put(other_refs, own_refs)


VMEM = pl.BlockSpec(memory_space=pltpu.VMEM)
SMEM = pl.BlockSpec(memory_space=pltpu.SMEM)
HBM = pl.BlockSpec(memory_space=pltpu.HBM)


def per_device(queries, keys, values, d_out, block_pos, block_mask):
    tokens, heads, depth = queries.shape
    kv_count = keys.shape[1]
    members = lax.axis_size("ctx") // SEQS
    sharers = GROUP // heads
    dims = Shape(tokens, heads, depth, members)
    head_index = lax.axis_index("head")
    kv_index = head_index // sharers
    f32, bf16 = jnp.float32, jnp.bfloat16
    sds = jax.ShapeDtypeStruct

    key_own = lax.dynamic_index_in_dim(keys, kv_index, 1, keepdims=False) if kv_count > 1 else keys[:, 0]
    value_own = lax.dynamic_index_in_dim(values, kv_index, 1, keepdims=False) if kv_count > 1 else values[:, 0]
    query_rows = queries.reshape(tokens * heads, depth)
    grad_rows = d_out.reshape(tokens * heads, depth)

    passed = pl.pallas_call(
        pick_kernel,
        out_shape=sds((tokens, depth), bf16),
        in_specs=[HBM] * 2,
        out_specs=VMEM,
        scratch_shapes=[pltpu.SemaphoreType.DMA((COPIES,))],
        compiler_params=pltpu.CompilerParams(vmem_limit_bytes=1 << 20),
        name="pick",
    )(*(pltpu.with_memory_space_constraint(operand, pltpu.HBM) for operand in (key_own, value_own)))
    near, swap = [], []
    for _ in range(members - 1):
        passed = shifted(passed, "ctx", SEQS)
        near.append(passed)
        swap.append(swapped(passed, "head", 1))
    near = near[0] if members == 2 else jnp.concatenate(near)
    swap = swap[0] if members == 2 else jnp.concatenate(swap)

    params = pltpu.CompilerParams(vmem_limit_bytes=16 << 20)
    blocks, rows = dims.blocks, dims.rows
    tile_flops = 2 * BLK * rows * depth

    def cost(tiles, dots):
        return pl.CostEstimate(
            flops=tiles * dots * tile_flops,
            bytes_accessed=4 * tokens * heads * depth,
            transcendentals=tiles * BLK * rows,
        )

    own_pairs = blocks + blocks * (blocks - 1) // 2 + 1
    (
        stats, bits, query_rows, grad_rows, key_own, value_own, query_cols, grad_cols, own_logits, own_dprobs,
    ) = pl.pallas_call(
        functools.partial(own_stats_kernel, dims),
        out_shape=(
            sds((blocks, 3, SUB, rows), f32),
            sds((2 * blocks, 128), jnp.int32),
            sds((tokens * heads, depth), bf16),
            sds((tokens * heads, depth), bf16),
            sds((tokens, depth), bf16),
            sds((tokens, depth), bf16),
            sds((blocks, depth, rows), bf16),
            sds((blocks, depth, rows), bf16),
            sds((own_pairs, BLK, rows), f32),
            sds((own_pairs, BLK, rows), f32),
        ),
        in_specs=[HBM] * 6,
        out_specs=(VMEM,) * 10,
        scratch_shapes=[
            pltpu.SMEM(PLAN, jnp.int32),
            pltpu.SMEM(block_pos.shape, jnp.int32),
            pltpu.SMEM(block_mask.shape, jnp.int32),
            pltpu.VMEM((blocks + 1, 3, SUB, rows), f32),
            pltpu.SemaphoreType.DMA((4,)),
            pltpu.SemaphoreType.DMA((2, blocks)),
        ],
        compiler_params=params,
        cost_estimate=cost(blocks * blocks, 2),
        name="own_stats",
    )(
        *(
            pltpu.with_memory_space_constraint(operand, pltpu.HBM)
            for operand in (block_pos, block_mask, query_rows, grad_rows, key_own, value_own)
        )
    )

    far = dims.far
    trips = blocks * pl.cdiv(far, 2)
    kept = trips if dims.keep_tiles else 1
    final, far_scores, keep_far, send_far = pl.pallas_call(
        functools.partial(far_kernel, dims),
        out_shape=(
            sds((blocks, 2, SUB, rows), f32),
            sds((trips, 2 * BLK, rows), bf16),
            sds((far * BLK, depth), f32),
            sds((far * BLK, depth), bf16),
        ),
        in_specs=[VMEM] * 8,
        out_specs=(VMEM,) * 4,
        scratch_shapes=[
            pltpu.SMEM(PLAN, jnp.int32),
            pltpu.VMEM((far * BLK, depth), bf16),
            pltpu.VMEM((far * BLK, depth), bf16),
            pltpu.VMEM((blocks + 1, 3, SUB, rows), f32),
            pltpu.VMEM((kept, 2 * BLK, rows), f32),
            pltpu.VMEM((kept, 2 * BLK, rows), f32),
            pltpu.VMEM((far + 1, BLK, depth), f32),
            pltpu.VMEM((far + 1, BLK, depth), f32),
        ],
        compiler_params=params,
        cost_estimate=cost(blocks * far, 4),
        name="far_part",
    )(bits, query_rows, grad_rows, query_cols, grad_cols, near, swap, stats)

    keep_own, send_own, own_scores = pl.pallas_call(
        functools.partial(own_sums_kernel, dims),
        out_shape=(
            sds((tokens, depth), f32),
            sds((tokens, depth), bf16),
            sds((own_pairs, BLK, rows), bf16),
        ),
        in_specs=[VMEM] * 6,
        out_specs=(VMEM,) * 3,
        scratch_shapes=[
            pltpu.SMEM(PLAN, jnp.int32),
            pltpu.VMEM((blocks + 1, BLK, depth), f32),
            pltpu.VMEM((blocks + 1, BLK, depth), f32),
        ],
        compiler_params=params,
        cost_estimate=cost(blocks * blocks, 2),
        name="own_sums",
    )(bits, query_rows, grad_rows, final, own_logits, own_dprobs)

    dq_own, far_cols = pl.pallas_call(
        functools.partial(own_queries_kernel, dims),
        out_shape=(sds((blocks + 1, depth, rows), f32), sds((far, depth, BLK), bf16)),
        in_specs=[VMEM] * 5,
        out_specs=(VMEM,) * 2,
        scratch_shapes=[
            pltpu.SMEM(PLAN, jnp.int32),
            pltpu.VMEM((blocks, depth, BLK), bf16),
        ],
        compiler_params=params,
        cost_estimate=cost(blocks * blocks, 1),
        name="own_queries",
    )(bits, key_own, near, swap, own_scores)

    dq = pl.pallas_call(
        functools.partial(queries_kernel, dims),
        out_shape=sds((tokens * heads, depth), bf16),
        in_specs=[VMEM] * 4,
        out_specs=HBM,
        scratch_shapes=[
            pltpu.SMEM(PLAN, jnp.int32),
            pltpu.VMEM((blocks, depth, rows), f32),
            pltpu.VMEM((tokens * heads, depth), bf16),
            pltpu.SemaphoreType.DMA((blocks,)),
        ],
        compiler_params=params,
        cost_estimate=cost(blocks * far, 1),
        name="queries",
    )(bits, far_cols, far_scores, dq_own)

    cuts = (0, tokens * 5 // 8, tokens)
    travel = bf16 if members == 2 else f32
    pair_far = keep_far + swapped(send_far, "head", 1).astype(f32)

    def far_piece(hop, index):
        return pair_far[(hop - 1) * tokens + cuts[index]:(hop - 1) * tokens + cuts[index + 1]]

    totals = [far_piece(1, index) for index in range(PIECES)]
    for hop in range(1, members):
        for index in range(PIECES):
            totals[index] = shifted(totals[index].astype(travel), "ctx", SEQS)
            if hop < members - 1:
                totals[index] = totals[index].astype(f32) + far_piece(hop + 1, index)
    swapped_own = swapped(send_own, "head", 1)
    pair_own = keep_own + swapped_own.astype(f32)
    others = []
    for index in range(PIECES):
        total = (totals[index].astype(f32) + pair_own[cuts[index]:cuts[index + 1]]).astype(bf16)
        bit = 2
        while bit < sharers:
            moved = swapped(total, "head", bit)
            total = (total.astype(f32) + moved.astype(f32)).astype(bf16)
            bit *= 2
        totals[index] = total
        others.append(swapped(total, "head", 1))
    d_keys, d_values = pl.pallas_call(
        place_kernel,
        out_shape=(sds((tokens, depth), bf16),) * 2,
        in_specs=[VMEM] * (2 * PIECES),
        out_specs=(HBM,) * 2,
        scratch_shapes=[pltpu.SemaphoreType.DMA((2, PIECES))],
        compiler_params=pltpu.CompilerParams(vmem_limit_bytes=1 << 20),
        name="place",
    )(*totals, *others)
    if kv_count > 1:
        groups = [[p + sharers * g for g in range(kv_count)] for p in range(sharers)]
        both = lax.all_gather(
            jnp.stack([d_keys, d_values]), "head", axis=2, axis_index_groups=groups
        )
        d_keys, d_values = both[0], both[1]
    else:
        d_keys, d_values = d_keys[:, None], d_values[:, None]
    return dq.reshape(tokens, heads, depth), d_keys, d_values


def solution(mesh):
    placed = (
        P("ctx", "head", None),
        P("ctx", None, None),
        P("ctx", None, None),
        P("ctx", "head", None),
        P(),
        P(),
    )
    return jax.shard_map(
        per_device,
        mesh=mesh,
        in_specs=placed,
        out_specs=(P("ctx", "head", None), P("ctx", None, None), P("ctx", None, None)),
        check_vma=False,
    )
```
